128 devices in a mesh: frames: 32 (over x, y, core), slabs: 4 (over z).
Axes of the slice: x: 4, y: 4, z: 4, core: 2. Of those that a mesh axis runs over, the one named last changes fastest.
Arguments:
- frame_pixels: float32 [256, 384, 1024], P('frames', 'slabs'), may hold values from -6 to 6
- bragg_mask: int32 [256, 384, 1024], P('frames', 'slabs'), may hold values 0 or 1
- interp: bfloat16 [4, 4096, 1024], P('slabs'), may hold values from -0.09375 to 0.09375
- block_list: int32 [256, 4, 96], P('frames', 'slabs'), may hold values from 0 to 4095, as said below
- owner_map: int32 [4, 4096], P('slabs'), may hold values from 0 to 4095, as said below
- mirror_pair: int32 [4, 128], P('slabs'), may hold values from 0 to 127, as said below
Outputs:
- merged: float32 [4, 4096, 1024], P('slabs', 'frames')
The draws below stay inside these ranges and needn't reach their ends.
Inputs may be any that keep to these rules, and one draw needn't show every extreme that they name: `block_list`: among the list entries of the frames of one frame group in one slab group, at most 48 name blocks whose position lies in one owner's range of 128 positions, and in every such set some owner receives exactly 48. `owner_map`: each row is a permutation of the block numbers. `mirror_pair`: each row is a permutation; the row of slab group s xor (2) is the inverse of the row of s, so pairs are mutual.
All inputs are finite; a program needn't handle non-finite values. No bound on the sum of `bragg_mask` on one device may be relied on, other than what follows from the above.
Results may differ from the reference program's by a relative error of at most 0.0029.
Values may be sent and summed in bfloat16 or wider, within the bound.
A program may use at most 128 MiB of HBM per device.

```python
import jax
import jax.numpy as jnp
from jax import lax

FRAME_DEV = 8
ROWS = 384
COLS = 1024
PANEL_ROWS = 4
RADIUS = 4
VOXELS = 1024
OWN_BLOCKS = 128
GROUPS = 32
SLABS = 4
FRAMES = 256
PANELS = 96
SLAB_BLOCKS = 4096
CAPACITY = 48


def block_table(key):
    table_rows = []
    for slab_index in range(SLABS):
        table_rows.append(jax.random.permutation(jax.random.fold_in(key, 100 + slab_index), SLAB_BLOCKS))
    return jnp.stack(table_rows).astype(jnp.int32)


def draw_owner_map(key, part):
    block_of = block_table(key)
    return jnp.argsort(block_of, axis=1).astype(jnp.int32)


def device_positions(device_key):
    key_slots = jax.random.fold_in(device_key, 1)
    key_favored = jax.random.fold_in(device_key, 2)
    key_shuffle = jax.random.fold_in(device_key, 3)
    key_within = jax.random.fold_in(device_key, 4)
    entry_count = FRAME_DEV * PANELS
    slots_all = jax.random.permutation(key_slots, GROUPS * CAPACITY)
    favored = jax.random.randint(key_favored, (), 0, GROUPS)
    priority = jnp.where(slots_all // CAPACITY == favored, 0, 1)
    sort_order = jnp.argsort(priority, stable=True)
    chosen = slots_all[sort_order][:entry_count]
    chosen = jax.random.permutation(key_shuffle, chosen)
    owner_index = chosen // CAPACITY
    slot_index = jax.random.randint(key_within, (entry_count,), 0, OWN_BLOCKS)
    return (owner_index * OWN_BLOCKS + slot_index).astype(jnp.int32)


def draw_block_list(key, part):
    block_of = block_table(key)
    device_keys = jax.random.split(jax.random.fold_in(key, 7), GROUPS * SLABS)
    positions = jax.vmap(device_positions)(device_keys)
    positions = positions.reshape(GROUPS, SLABS, FRAME_DEV * PANELS)
    slab_ids = jnp.arange(SLABS)[None, :, None]
    blocks = block_of[slab_ids, positions]
    blocks = blocks.reshape(GROUPS, SLABS, FRAME_DEV, PANELS)
    blocks = jnp.transpose(blocks, (0, 2, 1, 3)).reshape(FRAMES, SLABS, PANELS)
    return blocks.astype(jnp.int32)


def draw_mirror_pair(key, part):
    half_count = SLABS // 2
    table_rows = []
    for slab_index in range(SLABS):
        if slab_index < half_count:
            table_rows.append(jax.random.permutation(jax.random.fold_in(key, 300 + slab_index), OWN_BLOCKS))
        else:
            base_perm = jax.random.permutation(jax.random.fold_in(key, 300 + slab_index - half_count), OWN_BLOCKS)
            table_rows.append(jnp.argsort(base_perm))
    return jnp.stack(table_rows).astype(jnp.int32)


def place_ends(drawn, key, least, largest):
    place = [jax.random.randint(jax.random.fold_in(key, axis), (), 0, length) for axis, length in enumerate(drawn.shape)]
    longest = drawn.shape.index(max(drawn.shape))
    neighbour = place[:longest] + [(place[longest] + 1) % drawn.shape[longest]] + place[longest + 1:]
    return drawn.at[tuple(place)].set(least).at[tuple(neighbour)].set(largest)


def block_scale(stream_key, shape, pieces, least, largest):
    def one(axis_at, parts):
        heights = jax.random.uniform(jax.random.fold_in(jax.random.fold_in(stream_key, 6), axis_at), (parts,), jnp.float32, least / len(pieces), largest / len(pieces))
        return jnp.repeat(jnp.exp(heights), shape[axis_at] // parts).reshape((-1,) + (1,) * (len(shape) - axis_at - 1))

    loudness = one(*pieces[0])
    for cut in pieces[1:]:
        loudness = loudness * one(*cut)
    return loudness


def gaussian(own_key, shape, spread, most, shards=(), dtype=jnp.bfloat16):
    gain = block_scale(own_key, shape, shards, -0.22, 0.18) if shards else 1.0
    entries = jax.random.normal(own_key, shape, jnp.float32) * spread * gain
    return jnp.minimum(jnp.maximum(entries, -most), most).astype(dtype)


def setup_inputs(seed: int = 0) -> dict:
    seeds = jax.random.split(jax.random.key(seed), 7)
    frame_pixels = gaussian(seeds[0], (FRAMES, ROWS, COLS), 1.0, 6.0, ((0, 32), (1, 4)), jnp.float32)
    bragg_mask = place_ends((jax.random.randint(seeds[1], (FRAMES, ROWS, COLS), 0, 8) < 1).astype(jnp.int32), jax.random.fold_in(seeds[1], 1), 0, 1)
    interp = gaussian(seeds[2], (SLABS, PANEL_ROWS * COLS, VOXELS), (PANEL_ROWS * COLS) ** -0.5, 0.09375, ((0, 4),))
    block_list = draw_block_list(jax.random.fold_in(seeds[6], 71), 0)
    owner_map = draw_owner_map(jax.random.fold_in(seeds[6], 71), 0)
    mirror_pair = draw_mirror_pair(jax.random.fold_in(seeds[6], 71), 0)
    return {"frame_pixels": frame_pixels, "bragg_mask": bragg_mask, "interp": interp, "block_list": block_list, "owner_map": owner_map, "mirror_pair": mirror_pair}


EPSILON = 1e-05

def box_total(padded, row_count, col_count):
    box_width = 2 * RADIUS + 1
    row_sums = padded[:, 0:row_count, :]
    for offset in range(1, box_width):
        row_sums = row_sums + padded[:, offset:offset + row_count, :]
    full_sums = row_sums[:, :, 0:col_count]
    for offset in range(1, box_width):
        full_sums = full_sums + row_sums[:, :, offset:offset + col_count]
    return full_sums

def normalize(pixels, mask, row_padded):
    row_count = pixels.shape[1]
    col_count = pixels.shape[2]
    padded = jnp.pad(row_padded, ((0, 0), (0, 0), (RADIUS, RADIUS)))
    plain_sums = box_total(padded, row_count, col_count)
    square_sums = box_total(padded * padded, row_count, col_count)
    box_area = (2 * RADIUS + 1) * (2 * RADIUS + 1)
    box_mean = plain_sums / box_area
    box_var = square_sums / box_area - box_mean * box_mean
    scaled = (pixels - box_mean) * lax.rsqrt(box_var + EPSILON)
    return jnp.where(mask == 1, jnp.zeros_like(scaled), scaled).astype(jnp.bfloat16)

def reference(frame_pixels, bragg_mask, interp, block_list, owner_map, mirror_pair):
    weights_all = interp.astype(jnp.float32)
    pixel_groups = frame_pixels.reshape(GROUPS, FRAME_DEV, ROWS, COLS)
    mask_groups = bragg_mask.reshape(GROUPS, FRAME_DEV, ROWS, COLS)
    list_groups = block_list.reshape(GROUPS, FRAME_DEV, SLABS, PANELS)

    def accumulate(totals, inputs):
        pixels, mask, listed = inputs
        row_padded = jnp.pad(pixels, ((0, 0), (RADIUS, RADIUS), (0, 0)))
        corrected = normalize(pixels, mask, row_padded)
        panel_values = corrected.reshape(FRAME_DEV * PANELS, PANEL_ROWS * COLS).astype(jnp.float32)
        updated = []
        for slab_index in range(SLABS):
            terms = jnp.dot(panel_values, weights_all[slab_index], preferred_element_type=jnp.float32)
            position = owner_map[slab_index][listed[:, slab_index, :].reshape(-1)]
            added = jax.ops.segment_sum(terms, position, num_segments=SLAB_BLOCKS)
            updated.append(totals[slab_index] + added)
        return (jnp.stack(updated), None)
    start_sums = jnp.zeros((SLABS, SLAB_BLOCKS, VOXELS), jnp.float32)
    sums, _ = lax.scan(accumulate, start_sums, (pixel_groups, mask_groups, list_groups))
    half_count = SLABS // 2
    results = []
    for slab_index in range(SLABS):
        own_part = sums[slab_index].reshape(GROUPS, OWN_BLOCKS, VOXELS)
        partner = sums[slab_index ^ half_count].reshape(GROUPS, OWN_BLOCKS, VOXELS)
        paired = partner[:, mirror_pair[slab_index], :][:, :, ::-1]
        results.append((0.5 * (own_part + paired)).reshape(SLAB_BLOCKS, VOXELS))
    return jnp.stack(results)
```

```python
import jax
import jax.numpy as jnp
from jax import lax
from jax.experimental import pallas as pl
from jax.experimental.pallas import tpu as pltpu
from jax.sharding import PartitionSpec as P

MESH = pl.DeviceIdType.MESH
F32 = jnp.float32
BF16 = jnp.bfloat16
I32 = jnp.int32

EPSILON = 1e-05
AREA = 81
SIDE = 4
FRAMES = 8
ROWS = 96
COLS = 1024
VOX = 1024
HALF = 512
PIX = 4096
BAND = 16
STEPS = ROWS // BAND
ENTRIES = FRAMES * BAND
PART = ENTRIES // SIDE
OWN = 128


def spread(v, amount, axis):
    return pltpu.roll(v, amount % v.shape[axis], axis)


def box_rows(v):
    n = v.shape[0] - 8
    s2 = v[0 : n + 7] + v[1 : n + 8]
    s4 = s2[0 : n + 5] + s2[2 : n + 7]
    s8 = s4[0:n] + s4[4 : n + 4]
    return s8 + v[8 : n + 8]


def box_cols(h):
    h = jnp.concatenate([h, jnp.zeros((h.shape[0], 128), F32)], axis=1)
    s2 = h + spread(h, -1, 1)
    s4 = s2 + spread(s2, -2, 1)
    total = s4 + spread(s4, 4, 1) + spread(h, -4, 1)
    return total[:, :COLS]


def kernel(
    px_hbm, mk_hbm, w_hbm, bl_ref, om_ref, mp_ref, out_ref,
    px, mk, w2, corr, x_all, acc, o_all, e_all, acc2, table, pos, pall, tgt,
    hs, hr, s2, r2, fsum, tot, sib_in, mir_in, own,
    ld_sem, hs_sem, hr_sem, ps_sem, pr_sem, zs_sem, zr_sem, ss_sem, sr_sem,
    as_sem, ar_sem, bs_sem, br_sem, fs_sem, fr_sem,
):
    me = lax.axis_index("frames")
    z = lax.axis_index("slabs")
    core = me % 2
    y = (me // 2) % SIDE
    x = me // (2 * SIDE)
    a = jnp.where(core == 0, x, y)
    b = jnp.where(core == 0, y, x)
    sib_a = jnp.where(core == 0, y, x)

    def dev(xx, yy, cc, zz):
        return {"frames": (xx * SIDE + yy) * 2 + cc, "slabs": zz}

    def along_a(i):
        aa = (a + i) % SIDE
        return dev(jnp.where(core == 0, aa, x), jnp.where(core == 0, y, aa), core, z)

    def along_b(i):
        bb = (b + i) % SIDE
        return dev(jnp.where(core == 0, x, bb), jnp.where(core == 0, bb, y), core, z)

    z_up = (z + 1) % SIDE
    z_down = (z + SIDE - 1) % SIDE
    z_far = (z + 2) % SIDE
    up = dev(x, y, core, z_up)
    down = dev(x, y, core, z_down)
    sib = dev(x, y, 1 - core, z)

    def remote(src, dst, ssem, rsem, to):
        return pltpu.make_async_remote_copy(
            src_ref=src, dst_ref=dst, send_sem=ssem, recv_sem=rsem, device_id=to, device_id_type=MESH
        )

    load_px = pltpu.make_async_copy(px_hbm, px.at[:, pl.ds(8, ROWS), :], ld_sem.at[0])
    load_mk = pltpu.make_async_copy(mk_hbm, mk, ld_sem.at[1])
    load_w = [
        pltpu.make_async_copy(w_hbm.at[0, :, pl.ds(h * HALF, HALF)], w2.at[h], ld_sem.at[2 + h]) for h in range(2)
    ]
    load_px.start()
    load_mk.start()
    for c in load_w:
        c.start()

    barrier = pltpu.get_barrier_semaphore()
    partners = [up, down, sib, dev(x, y, core, z_far), dev(x, y, 1 - core, z_far)]
    for i in range(1, SIDE):
        for cc in range(2):
            partners.append(dev((x + i) % SIDE, y, cc, z))
            partners.append(dev(x, (y + i) % SIDE, cc, z))
    for to in partners:
        pl.semaphore_signal(barrier, inc=1, device_id=to, device_id_type=MESH)
    pl.semaphore_wait(barrier, len(partners))

    halo_up = remote(hs.at[0], hr.at[0], hs_sem.at[0], hr_sem.at[0], up)
    halo_down = remote(hs.at[1], hr.at[1], hs_sem.at[1], hr_sem.at[1], down)

    def z_direct(t, kind):
        ref = x_all.at[t, z]
        return remote(ref, ref, zs_sem.at[t, kind], zr_sem.at[t, kind], (up, down)[kind])

    def z_forward(t, kind):
        ref = x_all.at[t, (z_down, z_up)[kind], :, pl.ds(kind * (PIX // 2), PIX // 2)]
        return remote(ref, ref, zs_sem.at[t, 2 + kind], zr_sem.at[t, 2 + kind], (up, down)[kind])

    def sib_copy(t):
        return remote(o_all.at[t], e_all.at[t, sib_a, core], ss_sem.at[t], sr_sem.at[t], sib)

    def a_direct(t, kind):
        ref = e_all.at[t, a]
        return remote(ref, ref, as_sem.at[t, kind], ar_sem.at[t, kind], along_a((1, SIDE - 1)[kind]))

    def a_forward(t, kind):
        ref = e_all.at[t, (a + (SIDE - 1, 1)[kind]) % SIDE, kind]
        return remote(ref, ref, as_sem.at[t, 2 + kind], ar_sem.at[t, 2 + kind], along_a((1, SIDE - 1)[kind]))

    def b_copy(i):
        return remote(s2.at[i - 1], r2.at[i - 1], bs_sem.at[i - 1], br_sem.at[i - 1], along_b(i))

    pos_copies = [remote(pos, pall.at[sib_a * 2 + core], ps_sem.at[0], pr_sem.at[sib_a * 2 + core], sib)]
    for i in range(1, SIDE):
        pos_copies.append(
            remote(pos, pall.at[x * 2 + core], ps_sem.at[2 * i - 1], pr_sem.at[x * 2 + core], dev((x + i) % SIDE, y, 0, z))
        )
        pos_copies.append(
            remote(pos, pall.at[y * 2 + core], ps_sem.at[2 * i], pr_sem.at[y * 2 + core], dev(x, (y + i) % SIDE, 1, z))
        )

    def find_positions():
        lane = lax.broadcasted_iota(I32, (1, STEPS * ENTRIES), 1)
        step = lane >> 7
        e = lane & (ENTRIES - 1)
        band = jnp.where(step < 4, step + 1, jnp.where(step == 4, 0, 5))
        panel = (e >> 5) * 24 + band * 4 + (e & 3)
        frame = (e >> 2) & 7
        pick = (lax.broadcasted_iota(I32, (96, STEPS * ENTRIES), 0) == panel).astype(F32).astype(BF16)
        listed = bl_ref[:, 0, :]
        high = (listed >> 6).astype(F32).astype(BF16)
        low = (listed & 63).astype(F32).astype(BF16)
        is_frame = lax.broadcasted_iota(I32, (FRAMES, STEPS * ENTRIES), 0) == frame

        def taken(v):
            got = jnp.dot(v, pick, preferred_element_type=F32)
            return jnp.sum(jnp.where(is_frame, got, 0.0), axis=0, keepdims=True)

        block = (taken(high) * 64.0 + taken(low)).astype(I32)
        for i in range(32):
            table[i : i + 1, :] = om_ref[:, i * 128 : (i + 1) * 128]
        entry = table[...]
        in_row = (lax.broadcasted_iota(I32, (128, STEPS * ENTRIES), 0) == (block & 127)).astype(F32).astype(BF16)
        row_hit = lax.broadcasted_iota(I32, (32, STEPS * ENTRIES), 0) == (block >> 7)

        def looked(v):
            got = jnp.dot(v.astype(F32).astype(BF16), in_row, preferred_element_type=F32)
            return jnp.sum(jnp.where(row_hit, got, 0.0), axis=0, keepdims=True)

        found = (looked(entry >> 6) * 64.0 + looked(entry & 63)).astype(I32)
        pos[...] = jnp.zeros_like(pos)
        for i in range(STEPS):
            pos[i : i + 1, :] = found[:, i * 128 : (i + 1) * 128]
        pall[a * 2 + core] = pos[...]

    def make_targets():
        for k in range(2 * SIDE):
            at = pall[k]
            owner = at >> 7
            to_a = jnp.where(core == 0, owner >> 3, (owner >> 1) & 3)
            to_b = jnp.where(core == 0, (owner >> 1) & 3, owner >> 3)
            row = ((to_b * 2 + (owner & 1)) << 7) + (at & 127)
            tgt[:, k * 128 : (k + 1) * 128] = jnp.where(to_a == a, row, -1)

    def fill_halo():
        for f in range(FRAMES):
            top = hr[0, f // 2, (f % 2) * 4 : (f % 2) * 4 + 4, :]
            px[f, 4:8, :] = jnp.where(z > 0, top, 0.0)
            bottom = hr[1, f // 2, (f % 2) * 4 : (f % 2) * 4 + 4, :]
            px[f, 8 + ROWS : 12 + ROWS, :] = jnp.where(z < SIDE - 1, bottom, 0.0)

    def normalize(t):
        band = jnp.where(t < 4, t + 1, jnp.where(t == 4, 0, 5))
        row0 = pl.multiple_of(band * BAND, BAND)

        @pl.loop(0, FRAMES)
        def _(f):
            rows = px[f, pl.ds(row0, 2 * BAND), :]
            v = rows[4:28]
            mean = box_cols(box_rows(v)) * (1.0 / AREA)
            square = box_cols(box_rows(v * v)) * (1.0 / AREA)
            var = square - mean * mean
            scaled = (rows[8:24] - mean) * lax.rsqrt(var + EPSILON)
            kept = jnp.where(mk[f, pl.ds(row0, BAND), :] == 1, 0.0, scaled)
            for v in range(8):
                corr[v, pl.ds(pl.multiple_of(f * BAND, BAND), BAND), :] = kept[:, v * 128 : (v + 1) * 128]

        for r in range(4):
            for v in range(8):
                at = slice(r * COLS + v * 128, r * COLS + (v + 1) * 128)
                x_all[t, z, :, at] = corr[v, pl.ds(r, PART, stride=4), :].astype(BF16)

    def multiply(t):
        for own_half in range(2):
            h = core if own_half else 1 - core
            acc[...] = jnp.zeros_like(acc)

            @pl.loop(0, 4)
            def _(kc):
                at = pl.ds(pl.multiple_of(kc * 1024, 1024), 1024)
                left = x_all[t, :, :, at].reshape(ENTRIES, 1024)
                acc[...] += jnp.dot(left, w2[h, at, :], preferred_element_type=F32)

            if own_half:
                e_all[t, a, core] = acc[...].astype(BF16)
            else:
                o_all[t] = acc[...].astype(BF16)
                sib_copy(t).start()

    def add_entries(t):
        row = tgt[pl.ds(t, 1), :]

        @pl.loop(0, SIDE)
        def _(blk):
            at = pl.ds(pl.multiple_of(blk * 256, 256), 256)
            hit = (lax.broadcasted_iota(I32, (256, 1024), 0) + blk * 256) == row
            terms = e_all[t].reshape(1024, HALF)
            acc2[at, :] += jnp.dot(hit.astype(F32).astype(BF16), terms, preferred_element_type=F32)

    acc2[...] = jnp.zeros_like(acc2)
    load_px.wait()
    for f in range(FRAMES):
        at = slice((f % 2) * 4, (f % 2) * 4 + 4)
        hs[0, f // 2, at, :] = px[f, 4 + ROWS : 8 + ROWS, :]
        hs[1, f // 2, at, :] = px[f, 8:12, :]
    halo_up.start()
    halo_down.start()
    load_mk.wait()

    @pl.loop(0, STEPS + 4)
    def _(t):
        @pl.when(t == 4)
        def _():
            halo_up.wait_recv()
            halo_down.wait_recv()
            fill_halo()

        @pl.when(t < STEPS)
        def _():
            normalize(t)
            z_direct(t, 0).start()
            z_direct(t, 1).start()

        @pl.when(t == 0)
        def _():
            find_positions()
            for c in pos_copies:
                c.start()

        @pl.when((t >= 1) & (t < STEPS + 1))
        def _():
            for kind in range(2):
                z_direct(t - 1, kind).wait_recv()
                z_forward(t - 1, kind).start()

        @pl.when((t >= 3) & (t < STEPS + 3))
        def _():
            for kind in range(2):
                a_direct(t - 3, kind).wait_recv()
                a_forward(t - 3, kind).start()

        @pl.when(t == 2)
        def _():
            for c in load_w:
                c.wait()

        @pl.when((t >= 2) & (t < STEPS + 2))
        def _():
            for kind in range(2):
                z_forward(t - 2, kind).wait_recv()
            multiply(t - 2)

        @pl.when(t == 4)
        def _():
            def arrived(k):
                remote(pos, pall.at[k], ps_sem.at[0], pr_sem.at[k], sib).wait_recv()

            arrived(a * 2 + 1 - core)
            for i in range(1, SIDE):
                for g in range(2):
                    arrived(((a + i) % SIDE) * 2 + g)
            make_targets()

        @pl.when(t >= 4)
        def _():
            for kind in range(2):
                a_forward(t - 4, kind).wait_recv()
            add_entries(t - 4)

        @pl.when((t >= 2) & (t < STEPS + 2))
        def _():
            sib_copy(t - 2).wait_recv()
            a_direct(t - 2, 0).start()
            a_direct(t - 2, 1).start()

    for i in (2, 1, 3):
        at = pl.ds(pl.multiple_of(((b + i) % SIDE) * 256, 256), 256)
        s2[i - 1] = acc2[at, :].astype(BF16)
        b_copy(i).start()
    tot[...] = acc2[pl.ds(pl.multiple_of(b * 256, 256), 256), :]
    for i in (1, 3, 2):
        b_copy(i).wait_recv()
        tot[...] += r2[i - 1].astype(F32)
    for cc in range(2):
        fsum[cc] = tot[cc * OWN : (cc + 1) * OWN, :].astype(BF16)
    last = [
        remote(fsum.at[0], mir_in.at[core], fs_sem.at[0], fr_sem.at[core], dev(x, y, 0, z_far)),
        remote(fsum.at[1], mir_in.at[core], fs_sem.at[1], fr_sem.at[core], dev(x, y, 1, z_far)),
        remote(fsum.at[1 - core], sib_in, fs_sem.at[2], fr_sem.at[2], sib),
    ]
    for c in last:
        c.start()
    own[core] = tot[pl.ds(pl.multiple_of(core * OWN, OWN), OWN), :]
    pick = (lax.broadcasted_iota(I32, (OWN, OWN), 0) == mp_ref[...]).astype(F32).astype(BF16)
    flip = (
        lax.broadcasted_iota(I32, (OWN, OWN), 0) + lax.broadcasted_iota(I32, (OWN, OWN), 1) == OWN - 1
    ).astype(F32).astype(BF16)
    last[2].wait_recv()
    own[1 - core] = sib_in[...].astype(F32)
    for h in range(2):
        remote(fsum.at[0], mir_in.at[h], fs_sem.at[0], fr_sem.at[h], dev(x, y, 0, z_far)).wait_recv()
    for h in range(2):
        rows = lax.dot_general(pick, mir_in[1 - h], (((0,), (0,)), ((), ())), preferred_element_type=F32).astype(BF16)
        for v in range(4):
            turned = jnp.dot(rows[:, (3 - v) * OWN : (4 - v) * OWN], flip, preferred_element_type=F32)
            out_ref[0, :, h * HALF + v * OWN : h * HALF + (v + 1) * OWN] = 0.5 * (
                own[h, :, v * OWN : (v + 1) * OWN] + turned
            )

    halo_up.wait_send()
    halo_down.wait_send()
    for c in pos_copies:
        c.wait_send()

    @pl.loop(0, STEPS)
    def _(t):
        for kind in range(2):
            z_direct(t, kind).wait_send()
            z_forward(t, kind).wait_send()
            a_direct(t, kind).wait_send()
            a_forward(t, kind).wait_send()
        sib_copy(t).wait_send()

    for i in range(1, SIDE):
        b_copy(i).wait_send()
    for c in last:
        c.wait_send()


def shards(frame_pixels, bragg_mask, interp, block_list, owner_map, mirror_pair):
    vmem = pl.BlockSpec(memory_space=pltpu.VMEM)
    hbm = pl.BlockSpec(memory_space=pl.ANY)
    dma = pltpu.SemaphoreType.DMA
    return pl.pallas_call(
        kernel,
        out_shape=jax.ShapeDtypeStruct((1, OWN, VOX), F32),
        in_specs=[hbm, hbm, hbm, vmem, vmem, vmem],
        out_specs=vmem,
        scratch_shapes=[
            pltpu.VMEM((FRAMES, ROWS + 16, COLS), F32),
            pltpu.VMEM((FRAMES, ROWS, COLS), I32),
            pltpu.VMEM((2, PIX, HALF), BF16),
            pltpu.VMEM((8, ENTRIES, 128), F32),
            pltpu.VMEM((STEPS, SIDE, PART, PIX), BF16),
            pltpu.VMEM((ENTRIES, HALF), F32),
            pltpu.VMEM((STEPS, ENTRIES, HALF), BF16),
            pltpu.VMEM((STEPS, SIDE, 2, ENTRIES, HALF), BF16),
            pltpu.VMEM((1024, HALF), F32),
            pltpu.VMEM((32, 128), I32),
            pltpu.VMEM((8, 128), I32),
            pltpu.VMEM((2 * SIDE, 8, 128), I32),
            pltpu.VMEM((8, 1024), I32),
            pltpu.VMEM((2, FRAMES // 2, 8, COLS), F32),
            pltpu.VMEM((2, FRAMES // 2, 8, COLS), F32),
            pltpu.VMEM((3, 256, HALF), BF16),
            pltpu.VMEM((3, 256, HALF), BF16),
            pltpu.VMEM((2, OWN, HALF), BF16),
            pltpu.VMEM((256, HALF), F32),
            pltpu.VMEM((OWN, HALF), BF16),
            pltpu.VMEM((2, OWN, HALF), BF16),
            pltpu.VMEM((2, OWN, HALF), F32),
            dma((4,)),
            dma((2,)),
            dma((2,)),
            dma((7,)),
            dma((8,)),
            dma((STEPS, 4)),
            dma((STEPS, 4)),
            dma((STEPS,)),
            dma((STEPS,)),
            dma((STEPS, 4)),
            dma((STEPS, 4)),
            dma((3,)),
            dma((3,)),
            dma((3,)),
            dma((3,)),
        ],
        compiler_params=pltpu.CompilerParams(
            collective_id=0, has_side_effects=True, vmem_limit_bytes=60 * 1024 * 1024
        ),
    )(frame_pixels, bragg_mask, interp, block_list, owner_map, mirror_pair)


def solution(mesh):
    return jax.shard_map(
        shards,
        mesh=mesh,
        in_specs=(
            P("frames", "slabs", None),
            P("frames", "slabs", None),
            P("slabs", None, None),
            P("frames", "slabs", None),
            P("slabs", None),
            P("slabs", None),
        ),
        out_specs=P("slabs", "frames", None),
        check_vma=False,
    )
```

```python
import jax
import jax.numpy as jnp
from jax import lax
from jax.experimental import pallas as pl
from jax.experimental.pallas import tpu as pltpu
from jax.sharding import PartitionSpec as P

MESH = pl.DeviceIdType.MESH
F32 = jnp.float32
BF16 = jnp.bfloat16
I32 = jnp.int32

EPSILON = 1e-05
AREA = 81
SIDE = 4
FRAMES = 8
ROWS = 96
COLS = 1024
VOX = 1024
HALF = 512
QUART = 256
FIRST_ROWS = 56
PIX = 4096
BAND = 16
STEPS = ROWS // BAND
PART = FRAMES * BAND // 4
ENTRIES = 3 * PART
UNITS = STEPS + STEPS // 3
OWN = 128


def spread(v, amount, axis):
    return pltpu.roll(v, amount % v.shape[axis], axis)


def box_rows(v):
    n = v.shape[0] - 8
    s2 = v[0 : n + 7] + v[1 : n + 8]
    s4 = s2[0 : n + 5] + s2[2 : n + 7]
    s8 = s4[0:n] + s4[4 : n + 4]
    return s8 + v[8 : n + 8]


def box_cols(h):
    h = jnp.concatenate([h, jnp.zeros((h.shape[0], 128), F32)], axis=1)
    s2 = h + spread(h, -1, 1)
    s4 = s2 + spread(s2, -2, 1)
    total = s4 + spread(s4, 4, 1) + spread(h, -4, 1)
    return total[:, :COLS]


def kernel(
    px_hbm, mk_hbm, w_hbm, bl_ref, om_ref, mp_ref, out_ref,
    px, mk, w4, corr, x_all, acc, o_all, e_all, acc2, hits, table, pos, pall, tgt,
    hs, hr, s2, r2, fsum, tot, mir_in, own,
    ld_sem, lw_sem, hs_sem, hr_sem, ps_sem, pr_sem, zs_sem, zr_sem,
    as_sem, ar_sem, bs_sem, br_sem, fs_sem, fr_sem,
):
    me = lax.axis_index("frames")
    z = lax.axis_index("slabs")
    core = me % 2
    y = (me // 2) % SIDE
    x = me // (2 * SIDE)
    a = jnp.where(core == 0, x, y)
    b = jnp.where(core == 0, y, x)
    mine = a * 2 + core

    def dev(xx, yy, cc, zz):
        return {"frames": (xx * SIDE + yy) * 2 + cc, "slabs": zz}

    def along_b(i):
        bb = (b + i) % SIDE
        return dev(jnp.where(core == 0, x, bb), jnp.where(core == 0, bb, y), core, z)

    z_up = (z + 1) % SIDE
    z_down = (z + SIDE - 1) % SIDE
    z_far = (z + 2) % SIDE
    up = dev(x, y, core, z_up)
    down = dev(x, y, core, z_down)
    sib = dev(x, y, 1 - core, z)

    def along_a(i):
        aa = (a + i) % SIDE
        return dev(jnp.where(core == 0, aa, x), jnp.where(core == 0, y, aa), core, z)

    def along_other(i):
        aa = (b + i) % SIDE
        return dev(jnp.where(core == 0, x, aa), jnp.where(core == 0, aa, y), 1 - core, z)

    def remote(src, dst, ssem, rsem, to):
        return pltpu.make_async_remote_copy(
            src_ref=src, dst_ref=dst, send_sem=ssem, recv_sem=rsem, device_id=to, device_id_type=MESH
        )

    first = FIRST_ROWS
    loads = [
        pltpu.make_async_copy(px_hbm.at[:, pl.ds(0, first), :], px.at[:, pl.ds(8, first), :], ld_sem.at[0]),
        pltpu.make_async_copy(mk_hbm.at[:, pl.ds(0, first), :], mk.at[:, pl.ds(0, first), :], ld_sem.at[1]),
        pltpu.make_async_copy(
            px_hbm.at[:, pl.ds(first, ROWS - first), :], px.at[:, pl.ds(8 + first, ROWS - first), :], ld_sem.at[2]
        ),
        pltpu.make_async_copy(
            mk_hbm.at[:, pl.ds(first, ROWS - first), :], mk.at[:, pl.ds(first, ROWS - first), :], ld_sem.at[3]
        ),
    ]
    load_w = [
        pltpu.make_async_copy(w_hbm.at[0, :, pl.ds(i * QUART, QUART)], w4.at[i], lw_sem.at[i]) for i in range(4)
    ]
    for c in loads:
        c.start()

    barrier = pltpu.get_barrier_semaphore()
    partners = [up, down, sib, dev(x, y, core, z_far), dev(x, y, 1 - core, z_far)]
    for i in range(1, SIDE):
        for cc in range(2):
            partners.append(dev((x + i) % SIDE, y, cc, z))
            partners.append(dev(x, (y + i) % SIDE, cc, z))
    for to in partners:
        pl.semaphore_signal(barrier, inc=1, device_id=to, device_id_type=MESH)

    halo_up = remote(hs.at[0], hr.at[0], hs_sem.at[0], hr_sem.at[0], up)
    halo_down = remote(hs.at[1], hr.at[1], hs_sem.at[1], hr_sem.at[1], down)

    def z_direct(t, kind):
        return remote(x_all.at[t, 0], x_all.at[t, 1 + kind], zs_sem.at[t, kind], zr_sem.at[t, kind], (up, down)[kind])

    def z_forward(t, kind):
        at = pl.ds(kind * (PIX // 2), PIX // 2)
        src, dst = x_all.at[t, 1 + kind, :, at], x_all.at[STEPS + t // 3, t % 3, :, at]
        return remote(src, dst, zs_sem.at[t, 2 + kind], zr_sem.at[t, 2 + kind], (up, down)[kind])

    def entry_copies(t, q):
        copies = []
        for i in range(SIDE):
            slot = b * 2 + core
            copies.append(
                remote(o_all.at[t, q], e_all.at[t, q, slot], as_sem.at[t, q, i], ar_sem.at[t, q, slot], along_other(i))
            )
        for i in range(1, SIDE):
            ref = e_all.at[t, q, mine]
            copies.append(remote(ref, ref, as_sem.at[t, q, 3 + i], ar_sem.at[t, q, mine], along_a(i)))
        return copies

    def others():
        return [a * 2 + 1 - core] + [((a + i) % SIDE) * 2 + g for i in range(1, SIDE) for g in range(2)]

    def entries_arrived(t, q):
        for k in others():
            ref = e_all.at[t, q, k]
            remote(ref, ref, as_sem.at[t, q, 0], ar_sem.at[t, q, k], sib).wait_recv()

    def b_copy(i, q):
        return remote(s2.at[q, i - 1], r2.at[q, i - 1], bs_sem.at[q, i - 1], br_sem.at[q, i - 1], along_b(i))

    def last_copies(q):
        ref = tot.at[q, pl.ds(pl.multiple_of((1 - core) * OWN, OWN), OWN)]
        return [
            remote(fsum.at[q, 0], mir_in.at[core, q], fs_sem.at[q, 0], fr_sem.at[q, core], dev(x, y, 0, z_far)),
            remote(fsum.at[q, 1], mir_in.at[core, q], fs_sem.at[q, 1], fr_sem.at[q, core], dev(x, y, 1, z_far)),
            remote(ref, own.at[core, q], fs_sem.at[q, 2], fr_sem.at[q, 2], sib),
        ]

    pos_copies = []
    for i in range(SIDE):
        slot = b * 2 + core
        pos_copies.append(remote(pos, pall.at[slot], ps_sem.at[i], pr_sem.at[slot], along_other(i)))
    for i in range(1, SIDE):
        pos_copies.append(remote(pos, pall.at[mine], ps_sem.at[3 + i], pr_sem.at[mine], along_a(i)))

    def find_positions():
        lane = lax.broadcasted_iota(I32, (1, UNITS * 128), 1)
        unit = lane >> 7
        third = (lane >> 5) & 3
        near = unit < STEPS
        step = jnp.where(near, unit, (unit - STEPS) * 3 + third)
        band = jnp.where(step < 4, step + 1, jnp.where(step == 4, 0, 5))
        apart = jnp.where(near, jnp.where(third == 0, 0, jnp.where(third == 1, 3, 1)), 2)
        panel = ((z + apart) & 3) * 24 + band * 4 + (lane & 3)
        frame = (lane >> 2) & 7
        pick = (lax.broadcasted_iota(I32, (96, UNITS * 128), 0) == panel).astype(F32).astype(BF16)
        listed = bl_ref[:, 0, :]
        high = (listed >> 6).astype(F32).astype(BF16)
        low = (listed & 63).astype(F32).astype(BF16)
        is_frame = lax.broadcasted_iota(I32, (FRAMES, UNITS * 128), 0) == frame

        def taken(v):
            got = jnp.dot(v, pick, preferred_element_type=F32)
            return jnp.sum(jnp.where(is_frame, got, 0.0), axis=0, keepdims=True)

        block = (taken(high) * 64.0 + taken(low)).astype(I32)
        for i in range(32):
            table[i : i + 1, :] = om_ref[:, i * 128 : (i + 1) * 128]
        entry = table[...]
        in_row = (lax.broadcasted_iota(I32, (128, UNITS * 128), 0) == (block & 127)).astype(F32).astype(BF16)
        row_hit = lax.broadcasted_iota(I32, (32, UNITS * 128), 0) == (block >> 7)

        def looked(v):
            got = jnp.dot(v.astype(F32).astype(BF16), in_row, preferred_element_type=F32)
            return jnp.sum(jnp.where(row_hit, got, 0.0), axis=0, keepdims=True)

        found = (looked(entry >> 6) * 64.0 + looked(entry & 63)).astype(I32)
        for i in range(UNITS):
            pos[i : i + 1, :] = found[:, i * 128 : (i + 1) * 128]
        pall[mine] = pos[...]

    def make_targets():
        for k in range(2 * SIDE):
            at = pall[k]
            owner = at >> 7
            to_a = jnp.where(core == 0, owner >> 3, (owner >> 1) & 3)
            to_b = jnp.where(core == 0, (owner >> 1) & 3, owner >> 3)
            row = ((to_b * 2 + (owner & 1)) << 7) + (at & 127)
            tgt[:, k * ENTRIES : (k + 1) * ENTRIES] = jnp.where(to_a == a, row, -1)[:, :ENTRIES]

    def send_halo():
        for f in range(FRAMES):
            at = slice((f % 2) * 4, (f % 2) * 4 + 4)
            hs[0, f // 2, at, :] = px[f, 4 + ROWS : 8 + ROWS, :]
            hs[1, f // 2, at, :] = px[f, 8:12, :]
        halo_up.start()
        halo_down.start()

    def fill_halo():
        for f in range(FRAMES):
            top = hr[0, f // 2, (f % 2) * 4 : (f % 2) * 4 + 4, :]
            px[f, 4:8, :] = jnp.where(z > 0, top, 0.0)
            bottom = hr[1, f // 2, (f % 2) * 4 : (f % 2) * 4 + 4, :]
            px[f, 8 + ROWS : 12 + ROWS, :] = jnp.where(z < SIDE - 1, bottom, 0.0)

    def normalize(t):
        band = jnp.where(t < 4, t + 1, jnp.where(t == 4, 0, 5))
        row0 = pl.multiple_of(band * BAND, BAND)

        @pl.loop(0, FRAMES)
        def _(f):
            rows = px[f, pl.ds(row0, 2 * BAND), :]
            v = rows[4:28]
            mean = box_cols(box_rows(v)) * (1.0 / AREA)
            square = box_cols(box_rows(v * v)) * (1.0 / AREA)
            var = square - mean * mean
            scaled = (rows[8:24] - mean) * lax.rsqrt(var + EPSILON)
            kept = jnp.where(mk[f, pl.ds(row0, BAND), :] == 1, 0.0, scaled)
            for v in range(8):
                corr[v, pl.ds(pl.multiple_of(f * BAND, BAND), BAND), :] = kept[:, v * 128 : (v + 1) * 128]

        for r in range(4):
            for v in range(8):
                at = slice(r * COLS + v * 128, r * COLS + (v + 1) * 128)
                x_all[t, 0, :, at] = corr[v, pl.ds(r, PART, stride=4), :].astype(BF16)

    def z_start(t):
        for kind in range(2):
            z_direct(t, kind).start()

    def multiply(t):
        for q in range(2):
            for own_half in range(2):
                h = core if own_half else 1 - core
                part = jnp.dot(
                    x_all[t].reshape(ENTRIES, PIX), w4[h * 2 + q], preferred_element_type=F32
                ).astype(BF16)
                if own_half:
                    e_all[t, q, mine] = part
                else:
                    o_all[t, q] = part
            for c in entry_copies(t, q):
                c.start()

    def make_hits(t):
        row = tgt[pl.ds(t, 1), :]

        @pl.loop(0, SIDE)
        def _(blk):
            hit = (lax.broadcasted_iota(I32, (256, 2 * SIDE * ENTRIES), 0) + blk * 256) == row
            hits[blk] = hit.astype(F32).astype(BF16)

    def add_entries(t, q, blk):
        acc2[q, blk] += jnp.dot(
            hits[blk], e_all[t, q].reshape(2 * SIDE * ENTRIES, QUART), preferred_element_type=F32
        )

    def add_all(t):
        make_hits(t)
        for q in range(2):
            entries_arrived(t, q)
            sums = jnp.dot(
                hits[...].reshape(SIDE * 256, 2 * SIDE * ENTRIES),
                e_all[t, q].reshape(2 * SIDE * ENTRIES, QUART),
                preferred_element_type=F32,
            )
            acc2[q] += sums.reshape(SIDE, 256, QUART)

    acc2[...] = jnp.zeros_like(acc2)
    loads[0].wait()
    loads[1].wait()
    for c in load_w:
        c.start()

    @pl.loop(0, 2)
    def _(t):
        normalize(t)

    pl.semaphore_wait(barrier, len(partners))
    z_start(0)
    z_start(1)
    loads[2].wait()
    loads[3].wait()
    send_halo()
    find_positions()
    for c in pos_copies:
        c.start()

    @pl.loop(0, STEPS)
    def _(t):
        @pl.when(t == 2)
        def _():
            halo_up.wait_recv()
            halo_down.wait_recv()
            fill_halo()

        @pl.when(t < STEPS - 2)
        def _():
            normalize(t + 2)
            z_start(t + 2)

        for kind in range(2):
            z_direct(t, kind).wait_recv()
            z_forward(t, kind).start()

        @pl.when(t == 0)
        def _():
            for c in load_w:
                c.wait()

        multiply(t)

        @pl.when(t == 1)
        def _():
            for k in others():
                remote(pos, pall.at[k], ps_sem.at[0], pr_sem.at[k], sib).wait_recv()
            make_targets()

        @pl.when(t >= 1)
        def _():
            add_all(t - 1)

    end = UNITS - 1

    def far(u):
        for i in range(3):
            for kind in range(2):
                z_forward((u - STEPS) * 3 + i, kind).wait_recv()

    far(end - 1)
    multiply(end - 1)
    add_all(end - 2)
    far(end)
    multiply(end)
    add_all(end - 1)
    make_hits(end)

    for q in range(2):
        entries_arrived(end, q)
        for i in (2, 1, 3, 0):
            blk = (b + i) % SIDE
            add_entries(end, q, blk)
            if i:
                s2[q, i - 1] = acc2[q, blk].astype(BF16)
                b_copy(i, q).start()
    for q in range(2):
        for i in range(1, SIDE):
            b_copy(i, q).wait_recv()
        total = acc2[q, b] + (r2[q, 0].astype(F32) + r2[q, 1].astype(F32) + r2[q, 2].astype(F32))
        tot[q] = total
        for cc in range(2):
            fsum[q, cc] = total[cc * OWN : (cc + 1) * OWN, :].astype(BF16)
        for c in last_copies(q):
            c.start()
        own[core, q] = tot[q, pl.ds(pl.multiple_of(core * OWN, OWN), OWN), :]
    pick = (lax.broadcasted_iota(I32, (OWN, OWN), 0) == mp_ref[...]).astype(F32).astype(BF16)
    flip = (
        lax.broadcasted_iota(I32, (OWN, OWN), 0) + lax.broadcasted_iota(I32, (OWN, OWN), 1) == OWN - 1
    ).astype(F32).astype(BF16)
    for q in range(2):
        remote(own.at[0, q], own.at[0, q], fs_sem.at[q, 2], fr_sem.at[q, 2], sib).wait_recv()
        for h in range(2):
            ref = mir_in.at[h, q]
            remote(ref, ref, fs_sem.at[q, 0], fr_sem.at[q, h], dev(x, y, 0, z_far)).wait_recv()
        for h in range(2):
            rows = lax.dot_general(
                pick, mir_in[1 - h, q], (((0,), (0,)), ((), ())), preferred_element_type=F32
            ).astype(BF16)
            for v in range(2):
                turned = jnp.dot(rows[:, (1 - v) * OWN : (2 - v) * OWN], flip, preferred_element_type=F32)
                at = h * HALF + (1 - q) * QUART + v * OWN
                out_ref[0, :, at : at + OWN] = turned
    for q in range(2):
        for h in range(2):
            at = slice(h * HALF + q * QUART, h * HALF + (q + 1) * QUART)
            out_ref[0, :, at] = 0.5 * (own[h, q] + out_ref[0, :, at])

    halo_up.wait_send()
    halo_down.wait_send()
    for c in pos_copies:
        c.wait_send()

    @pl.loop(0, STEPS)
    def _(t):
        for kind in range(2):
            z_direct(t, kind).wait_send()
            z_forward(t, kind).wait_send()

    @pl.loop(0, UNITS)
    def _(t):
        for q in range(2):
            for c in entry_copies(t, q):
                c.wait_send()

    for q in range(2):
        for i in range(1, SIDE):
            b_copy(i, q).wait_send()
        for c in last_copies(q):
            c.wait_send()


def shards(frame_pixels, bragg_mask, interp, block_list, owner_map, mirror_pair):
    vmem = pl.BlockSpec(memory_space=pltpu.VMEM)
    hbm = pl.BlockSpec(memory_space=pl.ANY)
    dma = pltpu.SemaphoreType.DMA
    return pl.pallas_call(
        kernel,
        out_shape=jax.ShapeDtypeStruct((1, OWN, VOX), F32),
        in_specs=[hbm, hbm, hbm, vmem, vmem, vmem],
        out_specs=vmem,
        scratch_shapes=[
            pltpu.VMEM((FRAMES, ROWS + 16, COLS), F32),
            pltpu.VMEM((FRAMES, ROWS, COLS), I32),
            pltpu.VMEM((4, PIX, QUART), BF16),
            pltpu.VMEM((8, FRAMES * BAND, 128), F32),
            pltpu.VMEM((UNITS, 3, PART, PIX), BF16),
            pltpu.VMEM((ENTRIES, QUART), F32),
            pltpu.VMEM((UNITS, 2, ENTRIES, QUART), BF16),
            pltpu.VMEM((UNITS, 2, 2 * SIDE, ENTRIES, QUART), BF16),
            pltpu.VMEM((2, SIDE, 256, QUART), F32),
            pltpu.VMEM((SIDE, 256, 2 * SIDE * ENTRIES), BF16),
            pltpu.VMEM((32, 128), I32),
            pltpu.VMEM((8, 128), I32),
            pltpu.VMEM((2 * SIDE, 8, 128), I32),
            pltpu.VMEM((8, 2 * SIDE * ENTRIES), I32),
            pltpu.VMEM((2, FRAMES // 2, 8, COLS), F32),
            pltpu.VMEM((2, FRAMES // 2, 8, COLS), F32),
            pltpu.VMEM((2, 3, 256, QUART), BF16),
            pltpu.VMEM((2, 3, 256, QUART), BF16),
            pltpu.VMEM((2, 2, OWN, QUART), BF16),
            pltpu.VMEM((2, 256, QUART), F32),
            pltpu.VMEM((2, 2, OWN, QUART), BF16),
            pltpu.VMEM((2, 2, OWN, QUART), F32),
            dma((4,)),
            dma((4,)),
            dma((2,)),
            dma((2,)),
            dma((7,)),
            dma((8,)),
            dma((STEPS, 4)),
            dma((STEPS, 4)),
            dma((UNITS, 2, 7)),
            dma((UNITS, 2, 8)),
            dma((2, 3)),
            dma((2, 3)),
            dma((2, 3)),
            dma((2, 3)),
        ],
        compiler_params=pltpu.CompilerParams(
            collective_id=0, has_side_effects=True, vmem_limit_bytes=60 * 1024 * 1024
        ),
    )(frame_pixels, bragg_mask, interp, block_list, owner_map, mirror_pair)


def solution(mesh):
    return jax.shard_map(
        shards,
        mesh=mesh,
        in_specs=(
            P("frames", "slabs", None),
            P("frames", "slabs", None),
            P("slabs", None, None),
            P("frames", "slabs", None),
            P("slabs", None),
            P("slabs", None),
        ),
        out_specs=P("slabs", "frames", None),
        check_vma=False,
    )
```

```python
import jax
import jax.numpy as jnp
from jax import lax
from jax.experimental import pallas as pl
from jax.experimental.pallas import tpu as pltpu
from jax.sharding import PartitionSpec as P

MESH = pl.DeviceIdType.MESH
F32 = jnp.float32
BF16 = jnp.bfloat16
I32 = jnp.int32

EPSILON = 1e-05
AREA = 81
SIDE = 4
FRAMES = 8
ROWS = 96
COLS = 1024
VOX = 1024
HALF = 512
QUART = 256
FIRST_ROWS = 40
PIX = 4096
BAND = 16
STEPS = ROWS // BAND
PART = FRAMES * BAND // 4
ENTRIES = 3 * PART
UNITS = STEPS + STEPS // 3
OWN = 128
ALL = pl.ds(0, ENTRIES)
EARLY = pl.ds(0, 2 * PART)
LATE = pl.ds(2 * PART, PART)


def spread(v, amount, axis):
    return pltpu.roll(v, amount % v.shape[axis], axis)


def box_rows(v):
    n = v.shape[0] - 8
    s2 = v[0 : n + 7] + v[1 : n + 8]
    s4 = s2[0 : n + 5] + s2[2 : n + 7]
    s8 = s4[0:n] + s4[4 : n + 4]
    return s8 + v[8 : n + 8]


def box_cols(h):
    h = jnp.concatenate([h, jnp.zeros((h.shape[0], 128), F32)], axis=1)
    s2 = h + spread(h, -1, 1)
    s4 = s2 + spread(s2, -2, 1)
    total = s4 + spread(s4, 4, 1) + spread(h, -4, 1)
    return total[:, :COLS]


def kernel(
    px_hbm, mk_hbm, w_hbm, bl_ref, om_ref, mp_ref, out_ref,
    px, mk, w4, corr, x_all, acc, o_all, e_all, acc2, hits, table, pos, pall, tgt,
    hs, hr, s2, r2, fsum, tot, mir_in, own,
    ld_sem, lw_sem, hs_sem, hr_sem, ps_sem, pr_sem, zs_sem, zr_sem,
    as_sem, ar_sem, bs_sem, br_sem, fs_sem, fr_sem,
):
    me = lax.axis_index("frames")
    z = lax.axis_index("slabs")
    core = me % 2
    y = (me // 2) % SIDE
    x = me // (2 * SIDE)
    a = jnp.where(core == 0, x, y)
    b = jnp.where(core == 0, y, x)
    mine = a * 2 + core

    def dev(xx, yy, cc, zz):
        return {"frames": (xx * SIDE + yy) * 2 + cc, "slabs": zz}

    def along_b(i):
        bb = (b + i) % SIDE
        return dev(jnp.where(core == 0, x, bb), jnp.where(core == 0, bb, y), core, z)

    z_up = (z + 1) % SIDE
    z_down = (z + SIDE - 1) % SIDE
    z_far = (z + 2) % SIDE
    up = dev(x, y, core, z_up)
    down = dev(x, y, core, z_down)
    sib = dev(x, y, 1 - core, z)

    def along_a(i):
        aa = (a + i) % SIDE
        return dev(jnp.where(core == 0, aa, x), jnp.where(core == 0, y, aa), core, z)

    def along_other(i):
        aa = (b + i) % SIDE
        return dev(jnp.where(core == 0, x, aa), jnp.where(core == 0, aa, y), 1 - core, z)

    def remote(src, dst, ssem, rsem, to):
        return pltpu.make_async_remote_copy(
            src_ref=src, dst_ref=dst, send_sem=ssem, recv_sem=rsem, device_id=to, device_id_type=MESH
        )

    first = FIRST_ROWS
    loads = [
        pltpu.make_async_copy(px_hbm.at[:, pl.ds(0, first), :], px.at[:, pl.ds(8, first), :], ld_sem.at[0]),
        pltpu.make_async_copy(mk_hbm.at[:, pl.ds(0, first), :], mk.at[:, pl.ds(0, first), :], ld_sem.at[1]),
        pltpu.make_async_copy(
            px_hbm.at[:, pl.ds(first, ROWS - first), :], px.at[:, pl.ds(8 + first, ROWS - first), :], ld_sem.at[2]
        ),
        pltpu.make_async_copy(
            mk_hbm.at[:, pl.ds(first, ROWS - first), :], mk.at[:, pl.ds(first, ROWS - first), :], ld_sem.at[3]
        ),
    ]
    load_w = [
        pltpu.make_async_copy(w_hbm.at[0, :, pl.ds(i * QUART, QUART)], w4.at[i], lw_sem.at[i]) for i in range(4)
    ]
    for c in loads:
        c.start()

    barrier = pltpu.get_barrier_semaphore()
    partners = [up, down, sib, dev(x, y, core, z_far), dev(x, y, 1 - core, z_far)]
    for i in range(1, SIDE):
        for cc in range(2):
            partners.append(dev((x + i) % SIDE, y, cc, z))
            partners.append(dev(x, (y + i) % SIDE, cc, z))
    for to in partners:
        pl.semaphore_signal(barrier, inc=1, device_id=to, device_id_type=MESH)

    halo_up = remote(hs.at[0], hr.at[0], hs_sem.at[0], hr_sem.at[0], up)
    halo_down = remote(hs.at[1], hr.at[1], hs_sem.at[1], hr_sem.at[1], down)

    def z_direct(t, kind):
        return remote(x_all.at[t, 0], x_all.at[t, 1 + kind], zs_sem.at[t, kind], zr_sem.at[t, kind], (up, down)[kind])

    def z_forward(t, kind):
        at = pl.ds(kind * (PIX // 2), PIX // 2)
        src, dst = x_all.at[t, 1 + kind, :, at], x_all.at[STEPS + t // 3, t % 3, :, at]
        return remote(src, dst, zs_sem.at[t, 2 + kind], zr_sem.at[t, 2 + kind], (up, down)[kind])

    def entry_copies(n, t, at, q=None):
        cols, m = (pl.ds(0, 2), 0) if q is None else (pl.ds(q, 1), q)
        slot = b * 2 + core
        copies = []
        for i in range(SIDE):
            src, dst = o_all.at[t, cols, at], e_all.at[t, cols, slot, at]
            copies.append(remote(src, dst, as_sem.at[n, m, i], ar_sem.at[n, m, slot], along_other(i)))
        for i in range(1, SIDE):
            ref = e_all.at[t, cols, mine, at]
            copies.append(remote(ref, ref, as_sem.at[n, m, 3 + i], ar_sem.at[n, m, mine], along_a(i)))
        return copies

    def others():
        return [a * 2 + 1 - core] + [((a + i) % SIDE) * 2 + g for i in range(1, SIDE) for g in range(2)]

    def entries_arrived(n, t, at, q=None):
        cols, m = (pl.ds(0, 2), 0) if q is None else (pl.ds(q, 1), q)
        for k in others():
            ref = e_all.at[t, cols, k, at]
            remote(ref, ref, as_sem.at[n, m, 0], ar_sem.at[n, m, k], sib).wait_recv()

    def b_copy(i, q):
        return remote(s2.at[q, i - 1], r2.at[q, i - 1], bs_sem.at[q, i - 1], br_sem.at[q, i - 1], along_b(i))

    def last_copies(q):
        ref = tot.at[q, pl.ds(pl.multiple_of((1 - core) * OWN, OWN), OWN)]
        return [
            remote(fsum.at[q, 0], mir_in.at[core, q], fs_sem.at[q, 0], fr_sem.at[q, core], dev(x, y, 0, z_far)),
            remote(fsum.at[q, 1], mir_in.at[core, q], fs_sem.at[q, 1], fr_sem.at[q, core], dev(x, y, 1, z_far)),
            remote(ref, own.at[core, q], fs_sem.at[q, 2], fr_sem.at[q, 2], sib),
        ]

    pos_copies = []
    for i in range(SIDE):
        slot = b * 2 + core
        pos_copies.append(remote(pos, pall.at[slot], ps_sem.at[i], pr_sem.at[slot], along_other(i)))
    for i in range(1, SIDE):
        pos_copies.append(remote(pos, pall.at[mine], ps_sem.at[3 + i], pr_sem.at[mine], along_a(i)))

    def find_positions():
        lane = lax.broadcasted_iota(I32, (1, UNITS * 128), 1)
        unit = lane >> 7
        third = (lane >> 5) & 3
        near = unit < STEPS
        step = jnp.where(near, unit, (unit - STEPS) * 3 + third)
        band = jnp.where(step < 4, step + 1, jnp.where(step == 4, 0, 5))
        apart = jnp.where(near, jnp.where(third == 0, 0, jnp.where(third == 1, 3, 1)), 2)
        panel = ((z + apart) & 3) * 24 + band * 4 + (lane & 3)
        frame = (lane >> 2) & 7
        pick = (lax.broadcasted_iota(I32, (96, UNITS * 128), 0) == panel).astype(F32).astype(BF16)
        listed = bl_ref[:, 0, :]
        high = (listed >> 6).astype(F32).astype(BF16)
        low = (listed & 63).astype(F32).astype(BF16)
        is_frame = lax.broadcasted_iota(I32, (FRAMES, UNITS * 128), 0) == frame

        def taken(v):
            got = jnp.dot(v, pick, preferred_element_type=F32)
            return jnp.sum(jnp.where(is_frame, got, 0.0), axis=0, keepdims=True)

        block = (taken(high) * 64.0 + taken(low)).astype(I32)
        for i in range(32):
            table[i : i + 1, :] = om_ref[:, i * 128 : (i + 1) * 128]
        entry = table[...]
        in_row = (lax.broadcasted_iota(I32, (128, UNITS * 128), 0) == (block & 127)).astype(F32).astype(BF16)
        row_hit = lax.broadcasted_iota(I32, (32, UNITS * 128), 0) == (block >> 7)

        def looked(v):
            got = jnp.dot(v.astype(F32).astype(BF16), in_row, preferred_element_type=F32)
            return jnp.sum(jnp.where(row_hit, got, 0.0), axis=0, keepdims=True)

        found = (looked(entry >> 6) * 64.0 + looked(entry & 63)).astype(I32)
        for i in range(UNITS):
            pos[i : i + 1, :] = found[:, i * 128 : (i + 1) * 128]
        pall[mine] = pos[...]

    def make_targets():
        for k in range(2 * SIDE):
            at = pall[k]
            owner = at >> 7
            to_a = jnp.where(core == 0, owner >> 3, (owner >> 1) & 3)
            to_b = jnp.where(core == 0, (owner >> 1) & 3, owner >> 3)
            row = ((to_b * 2 + (owner & 1)) << 7) + (at & 127)
            tgt[:, k * ENTRIES : (k + 1) * ENTRIES] = jnp.where(to_a == a, row, -1)[:, :ENTRIES]

    def send_halo():
        for f in range(FRAMES):
            at = slice((f % 2) * 4, (f % 2) * 4 + 4)
            hs[0, f // 2, at, :] = px[f, 4 + ROWS : 8 + ROWS, :]
            hs[1, f // 2, at, :] = px[f, 8:12, :]
        halo_up.start()
        halo_down.start()

    def fill_halo():
        for f in range(FRAMES):
            top = hr[0, f // 2, (f % 2) * 4 : (f % 2) * 4 + 4, :]
            px[f, 4:8, :] = jnp.where(z > 0, top, 0.0)
            bottom = hr[1, f // 2, (f % 2) * 4 : (f % 2) * 4 + 4, :]
            px[f, 8 + ROWS : 12 + ROWS, :] = jnp.where(z < SIDE - 1, bottom, 0.0)

    def normalize(t):
        band = jnp.where(t < 4, t + 1, jnp.where(t == 4, 0, 5))
        row0 = pl.multiple_of(band * BAND, BAND)

        @pl.loop(0, FRAMES)
        def _(f):
            rows = px[f, pl.ds(row0, 2 * BAND), :]
            v = rows[4:28]
            mean = box_cols(box_rows(v)) * (1.0 / AREA)
            square = box_cols(box_rows(v * v)) * (1.0 / AREA)
            var = square - mean * mean
            scaled = (rows[8:24] - mean) * lax.rsqrt(var + EPSILON)
            kept = jnp.where(mk[f, pl.ds(row0, BAND), :] == 1, 0.0, scaled)
            for v in range(8):
                corr[v, pl.ds(pl.multiple_of(f * BAND, BAND), BAND), :] = kept[:, v * 128 : (v + 1) * 128]

        for r in range(4):
            for v in range(8):
                at = slice(r * COLS + v * 128, r * COLS + (v + 1) * 128)
                x_all[t, 0, :, at] = corr[v, pl.ds(r, PART, stride=4), :].astype(BF16)

    def z_start(t):
        for kind in range(2):
            z_direct(t, kind).start()

    def multiply(t, blocks=(0, 3), sets=None):
        low, high = blocks
        at = slice(low * PART, high * PART)
        left = x_all.at[t, low:high]
        for q in range(2):
            for own_half in range(2):
                h = core if own_half else 1 - core
                part = jnp.dot(
                    left[...].reshape((high - low) * PART, PIX), w4[h * 2 + q], preferred_element_type=F32
                ).astype(BF16)
                if own_half:
                    e_all[t, q, mine, at] = part
                else:
                    o_all[t, q, at] = part
            if sets:
                for c in entry_copies(sets[q][0], t, sets[q][1], q):
                    c.start()

    def send_entries(copies):
        for c in copies:
            c.start()

    def make_hits(t):
        row = tgt[pl.ds(t, 1), :]

        @pl.loop(0, SIDE)
        def _(blk):
            hit = (lax.broadcasted_iota(I32, (256, 2 * SIDE * ENTRIES), 0) + blk * 256) == row
            hits[blk] = hit.astype(F32).astype(BF16)

    def add_entries(t, q, blk):
        acc2[q, blk] += jnp.dot(
            hits[blk], e_all[t, q].reshape(2 * SIDE * ENTRIES, QUART), preferred_element_type=F32
        )

    def add_unit(t, q):
        sums = jnp.dot(
            hits[...].reshape(SIDE * 256, 2 * SIDE * ENTRIES),
            e_all[t, q].reshape(2 * SIDE * ENTRIES, QUART),
            preferred_element_type=F32,
        )
        acc2[q] += sums.reshape(SIDE, 256, QUART)

    def add_all(t):
        make_hits(t)
        for q in range(2):
            entries_arrived(t, t, ALL, q)
            add_unit(t, q)

    loads[0].wait()
    loads[1].wait()
    normalize(0)
    pl.semaphore_wait(barrier, len(partners))
    z_start(0)
    loads[2].wait()
    loads[3].wait()
    for c in load_w:
        c.start()
    normalize(1)
    z_start(1)
    acc2[...] = jnp.zeros_like(acc2)
    send_halo()
    find_positions()
    for c in pos_copies:
        c.start()

    @pl.loop(2, STEPS)
    def _(t):
        @pl.when(t == 4)
        def _():
            halo_up.wait_recv()
            halo_down.wait_recv()
            fill_halo()

        normalize(t)
        z_start(t)

    @pl.loop(0, STEPS)
    def _(t):
        for kind in range(2):
            z_direct(t, kind).wait_recv()

        @pl.when(t < STEPS - 1)
        def _():
            for kind in range(2):
                z_forward(t, kind).start()

        @pl.when(t == 0)
        def _():
            for c in load_w:
                c.wait()

        multiply(t, sets=[(t, ALL)] * 2)

        @pl.when(t == 1)
        def _():
            for k in others():
                remote(pos, pall.at[k], ps_sem.at[0], pr_sem.at[k], sib).wait_recv()
            make_targets()

        @pl.when(t >= 1)
        def _():
            add_all(t - 1)

    end = UNITS - 1

    def far(u, low, high):
        for i in range(low, high):
            for kind in range(2):
                z_forward((u - STEPS) * 3 + i, kind).wait_recv()

    far(end - 1, 0, 3)
    multiply(end - 1, sets=[(end - 1, ALL)] * 2)
    for kind in range(2):
        z_forward(STEPS - 3, kind).wait_send()
        z_forward(STEPS - 1, kind).start()
    add_all(end - 2)
    far(end, 0, 2)
    multiply(end, (0, 2))
    send_entries(entry_copies(end, end, EARLY))
    far(end, 2, 3)
    multiply(end, (2, 3), [(end + 1, LATE)] * 2)
    add_all(end - 1)
    make_hits(end)
    entries_arrived(end, end, EARLY)

    for q in range(2):
        entries_arrived(end + 1, end, LATE, q)
        for i in (2, 1, 3, 0):
            blk = (b + i) % SIDE
            add_entries(end, q, blk)
            if i:
                s2[q, i - 1] = acc2[q, blk].astype(BF16)
                b_copy(i, q).start()
    for q in range(2):
        for i in range(1, SIDE):
            b_copy(i, q).wait_recv()
        total = acc2[q, b] + (r2[q, 0].astype(F32) + r2[q, 1].astype(F32) + r2[q, 2].astype(F32))
        tot[q] = total
        for cc in range(2):
            fsum[q, cc] = total[cc * OWN : (cc + 1) * OWN, :].astype(BF16)
        for c in last_copies(q):
            c.start()
        own[core, q] = tot[q, pl.ds(pl.multiple_of(core * OWN, OWN), OWN), :]
    pick = (lax.broadcasted_iota(I32, (OWN, OWN), 0) == mp_ref[...]).astype(F32).astype(BF16)
    flip = (
        lax.broadcasted_iota(I32, (OWN, OWN), 0) + lax.broadcasted_iota(I32, (OWN, OWN), 1) == OWN - 1
    ).astype(F32).astype(BF16)
    for q in range(2):
        remote(own.at[0, q], own.at[0, q], fs_sem.at[q, 2], fr_sem.at[q, 2], sib).wait_recv()
        for h in range(2):
            ref = mir_in.at[h, q]
            remote(ref, ref, fs_sem.at[q, 0], fr_sem.at[q, h], dev(x, y, 0, z_far)).wait_recv()
        for h in range(2):
            rows = lax.dot_general(
                pick, mir_in[1 - h, q], (((0,), (0,)), ((), ())), preferred_element_type=F32
            ).astype(BF16)
            for v in range(2):
                turned = jnp.dot(rows[:, (1 - v) * OWN : (2 - v) * OWN], flip, preferred_element_type=F32)
                at = h * HALF + (1 - q) * QUART + v * OWN
                out_ref[0, :, at : at + OWN] = turned
    for q in range(2):
        for h in range(2):
            at = slice(h * HALF + q * QUART, h * HALF + (q + 1) * QUART)
            out_ref[0, :, at] = 0.5 * (own[h, q] + out_ref[0, :, at])

    halo_up.wait_send()
    halo_down.wait_send()
    for c in pos_copies:
        c.wait_send()

    @pl.loop(0, STEPS)
    def _(t):
        for kind in range(2):
            z_direct(t, kind).wait_send()

        @pl.when(t != STEPS - 3)
        def _():
            for kind in range(2):
                z_forward(t, kind).wait_send()

    @pl.loop(0, end)
    def _(t):
        for q in range(2):
            for c in entry_copies(t, t, ALL, q):
                c.wait_send()

    for c in entry_copies(end, end, EARLY):
        c.wait_send()
    for q in range(2):
        for c in entry_copies(end + 1, end, LATE, q):
            c.wait_send()

    for q in range(2):
        for i in range(1, SIDE):
            b_copy(i, q).wait_send()
        for c in last_copies(q):
            c.wait_send()


def shards(frame_pixels, bragg_mask, interp, block_list, owner_map, mirror_pair):
    vmem = pl.BlockSpec(memory_space=pltpu.VMEM)
    hbm = pl.BlockSpec(memory_space=pl.ANY)
    dma = pltpu.SemaphoreType.DMA
    return pl.pallas_call(
        kernel,
        out_shape=jax.ShapeDtypeStruct((1, OWN, VOX), F32),
        in_specs=[hbm, hbm, hbm, vmem, vmem, vmem],
        out_specs=vmem,
        scratch_shapes=[
            pltpu.VMEM((FRAMES, ROWS + 16, COLS), F32),
            pltpu.VMEM((FRAMES, ROWS, COLS), I32),
            pltpu.VMEM((4, PIX, QUART), BF16),
            pltpu.VMEM((8, FRAMES * BAND, 128), F32),
            pltpu.VMEM((UNITS, 3, PART, PIX), BF16),
            pltpu.VMEM((ENTRIES, QUART), F32),
            pltpu.VMEM((UNITS, 2, ENTRIES, QUART), BF16),
            pltpu.VMEM((UNITS, 2, 2 * SIDE, ENTRIES, QUART), BF16),
            pltpu.VMEM((2, SIDE, 256, QUART), F32),
            pltpu.VMEM((SIDE, 256, 2 * SIDE * ENTRIES), BF16),
            pltpu.VMEM((32, 128), I32),
            pltpu.VMEM((8, 128), I32),
            pltpu.VMEM((2 * SIDE, 8, 128), I32),
            pltpu.VMEM((8, 2 * SIDE * ENTRIES), I32),
            pltpu.VMEM((2, FRAMES // 2, 8, COLS), F32),
            pltpu.VMEM((2, FRAMES // 2, 8, COLS), F32),
            pltpu.VMEM((2, 3, 256, QUART), BF16),
            pltpu.VMEM((2, 3, 256, QUART), BF16),
            pltpu.VMEM((2, 2, OWN, QUART), BF16),
            pltpu.VMEM((2, 256, QUART), F32),
            pltpu.VMEM((2, 2, OWN, QUART), BF16),
            pltpu.VMEM((2, 2, OWN, QUART), F32),
            dma((4,)),
            dma((4,)),
            dma((2,)),
            dma((2,)),
            dma((7,)),
            dma((8,)),
            dma((STEPS, 4)),
            dma((STEPS, 4)),
            dma((UNITS + 1, 2, 7)),
            dma((UNITS + 1, 2, 8)),
            dma((2, 3)),
            dma((2, 3)),
            dma((2, 3)),
            dma((2, 3)),
        ],
        compiler_params=pltpu.CompilerParams(
            collective_id=0, has_side_effects=True, vmem_limit_bytes=60 * 1024 * 1024
        ),
    )(frame_pixels, bragg_mask, interp, block_list, owner_map, mirror_pair)


def solution(mesh):
    return jax.shard_map(
        shards,
        mesh=mesh,
        in_specs=(
            P("frames", "slabs", None),
            P("frames", "slabs", None),
            P("slabs", None, None),
            P("frames", "slabs", None),
            P("slabs", None),
            P("slabs", None),
        ),
        out_specs=P("slabs", "frames", None),
        check_vma=False,
    )
```

```python
import jax
import jax.numpy as jnp
from jax import lax
from jax.experimental import pallas as pl
from jax.experimental.pallas import tpu as pltpu
from jax.sharding import PartitionSpec as P

MESH = pl.DeviceIdType.MESH
F32 = jnp.float32
BF16 = jnp.bfloat16
I32 = jnp.int32

EPSILON = 1e-05
AREA = 81
SIDE = 4
FRAMES = 8
ROWS = 96
COLS = 1024
VOX = 1024
HALF = 512
QUART = 256
FIRST_ROWS = 40
PIX = 4096
BAND = 16
STEPS = ROWS // BAND
PART = FRAMES * BAND // 4
ENTRIES = 3 * PART
UNITS = STEPS + STEPS // 3
OWN = 128
ALL = pl.ds(0, ENTRIES)
EARLY = pl.ds(0, 2 * PART)
LATE = pl.ds(2 * PART, PART)


def spread(v, amount, axis):
    return pltpu.roll(v, amount % v.shape[axis], axis)


def box_rows(v):
    n = v.shape[0] - 8
    s2 = v[0 : n + 7] + v[1 : n + 8]
    s4 = s2[0 : n + 5] + s2[2 : n + 7]
    s8 = s4[0:n] + s4[4 : n + 4]
    return s8 + v[8 : n + 8]


def box_cols(h):
    h = jnp.concatenate([h, jnp.zeros((h.shape[0], 128), F32)], axis=1)
    s2 = h + spread(h, -1, 1)
    s4 = s2 + spread(s2, -2, 1)
    total = s4 + spread(s4, 4, 1) + spread(h, -4, 1)
    return total[:, :COLS]


def kernel(
    px_hbm, mk_hbm, w_hbm, bl_ref, om_ref, mp_ref, out_ref,
    px, mk, w4, corr, x_all, acc, o_all, e_all, acc2, hits, table, pos, pall, tgt, early_tgt, late_tgt, late_hits,
    hs, hr, s2, r2, fsum, tot, mir_in, own,
    ld_sem, lw_sem, hs_sem, hr_sem, ps_sem, pr_sem, zs_sem, zr_sem,
    as_sem, ar_sem, bs_sem, br_sem, fs_sem, fr_sem,
):
    me = lax.axis_index("frames")
    z = lax.axis_index("slabs")
    core = me % 2
    y = (me // 2) % SIDE
    x = me // (2 * SIDE)
    a = jnp.where(core == 0, x, y)
    b = jnp.where(core == 0, y, x)
    mine = a * 2 + core

    def dev(xx, yy, cc, zz):
        return {"frames": (xx * SIDE + yy) * 2 + cc, "slabs": zz}

    def along_b(i):
        bb = (b + i) % SIDE
        return dev(jnp.where(core == 0, x, bb), jnp.where(core == 0, bb, y), core, z)

    z_up = (z + 1) % SIDE
    z_down = (z + SIDE - 1) % SIDE
    z_far = (z + 2) % SIDE
    up = dev(x, y, core, z_up)
    down = dev(x, y, core, z_down)
    sib = dev(x, y, 1 - core, z)

    def along_a(i):
        aa = (a + i) % SIDE
        return dev(jnp.where(core == 0, aa, x), jnp.where(core == 0, y, aa), core, z)

    def along_other(i):
        aa = (b + i) % SIDE
        return dev(jnp.where(core == 0, x, aa), jnp.where(core == 0, aa, y), 1 - core, z)

    def remote(src, dst, ssem, rsem, to):
        return pltpu.make_async_remote_copy(
            src_ref=src, dst_ref=dst, send_sem=ssem, recv_sem=rsem, device_id=to, device_id_type=MESH
        )

    first = FIRST_ROWS
    loads = [
        pltpu.make_async_copy(px_hbm.at[:, pl.ds(0, first), :], px.at[:, pl.ds(8, first), :], ld_sem.at[0]),
        pltpu.make_async_copy(mk_hbm.at[:, pl.ds(0, first), :], mk.at[:, pl.ds(0, first), :], ld_sem.at[1]),
        pltpu.make_async_copy(
            px_hbm.at[:, pl.ds(first, ROWS - first), :], px.at[:, pl.ds(8 + first, ROWS - first), :], ld_sem.at[2]
        ),
        pltpu.make_async_copy(
            mk_hbm.at[:, pl.ds(first, ROWS - first), :], mk.at[:, pl.ds(first, ROWS - first), :], ld_sem.at[3]
        ),
    ]
    load_w = [
        pltpu.make_async_copy(w_hbm.at[0, :, pl.ds(i * QUART, QUART)], w4.at[i], lw_sem.at[i]) for i in range(4)
    ]
    for c in loads:
        c.start()

    barrier = pltpu.get_barrier_semaphore()
    partners = [up, down, sib, dev(x, y, core, z_far), dev(x, y, 1 - core, z_far)]
    for i in range(1, SIDE):
        for cc in range(2):
            partners.append(dev((x + i) % SIDE, y, cc, z))
            partners.append(dev(x, (y + i) % SIDE, cc, z))
    for to in partners:
        pl.semaphore_signal(barrier, inc=1, device_id=to, device_id_type=MESH)

    halo_up = remote(hs.at[0], hr.at[0], hs_sem.at[0], hr_sem.at[0], up)
    halo_down = remote(hs.at[1], hr.at[1], hs_sem.at[1], hr_sem.at[1], down)

    end = UNITS - 1

    def z_direct(t, kind):
        return remote(x_all.at[t, 0], x_all.at[t, 1 + kind], zs_sem.at[t, kind], zr_sem.at[t, kind], (up, down)[kind])

    def z_forward(t, kind):
        at = pl.ds(kind * (PIX // 2), PIX // 2)
        src, dst = x_all.at[t, 1 + kind, :, at], x_all.at[STEPS + t // 3, t % 3, :, at]
        return remote(src, dst, zs_sem.at[t, 2 + kind], zr_sem.at[t, 2 + kind], (up, down)[kind])

    def entry_copies(n, t, at, q=None):
        cols, m = (pl.ds(0, 2), 0) if q is None else (pl.ds(q, 1), q)
        slot = b * 2 + core
        copies = []
        for i in range(SIDE):
            src, dst = o_all.at[t, cols, at], e_all.at[t, cols, slot, at]
            copies.append(remote(src, dst, as_sem.at[n, m, i], ar_sem.at[n, m, slot], along_other(i)))
        for i in range(1, SIDE):
            ref = e_all.at[t, cols, mine, at]
            copies.append(remote(ref, ref, as_sem.at[n, m, 3 + i], ar_sem.at[n, m, mine], along_a(i)))
        return copies

    def others():
        return [a * 2 + 1 - core] + [((a + i) % SIDE) * 2 + g for i in range(1, SIDE) for g in range(2)]

    def entries_arrived(n, t, at, q=None):
        cols, m = (pl.ds(0, 2), 0) if q is None else (pl.ds(q, 1), q)
        for k in others():
            ref = e_all.at[t, cols, k, at]
            remote(ref, ref, as_sem.at[n, m, 0], ar_sem.at[n, m, k], sib).wait_recv()

    def b_copy(i, q):
        return remote(s2.at[q, i - 1], r2.at[q, i - 1], bs_sem.at[q, i - 1], br_sem.at[q, i - 1], along_b(i))

    def last_copies(q):
        ref = tot.at[q, pl.ds(pl.multiple_of((1 - core) * OWN, OWN), OWN)]
        return [
            remote(fsum.at[q, 0], mir_in.at[core, q], fs_sem.at[q, 0], fr_sem.at[q, core], dev(x, y, 0, z_far)),
            remote(fsum.at[q, 1], mir_in.at[core, q], fs_sem.at[q, 1], fr_sem.at[q, core], dev(x, y, 1, z_far)),
            remote(ref, own.at[core, q], fs_sem.at[q, 2], fr_sem.at[q, 2], sib),
        ]

    pos_copies = []
    for i in range(SIDE):
        slot = b * 2 + core
        pos_copies.append(remote(pos, pall.at[slot], ps_sem.at[i], pr_sem.at[slot], along_other(i)))
    for i in range(1, SIDE):
        pos_copies.append(remote(pos, pall.at[mine], ps_sem.at[3 + i], pr_sem.at[mine], along_a(i)))

    def find_positions():
        lane = lax.broadcasted_iota(I32, (1, UNITS * 128), 1)
        unit = lane >> 7
        third = (lane >> 5) & 3
        near = unit < STEPS
        step = jnp.where(near, unit, (unit - STEPS) * 3 + third)
        band = jnp.where(step < 4, step + 1, jnp.where(step == 4, 0, 5))
        apart = jnp.where(near, jnp.where(third == 0, 0, jnp.where(third == 1, 3, 1)), 2)
        panel = ((z + apart) & 3) * 24 + band * 4 + (lane & 3)
        frame = (lane >> 2) & 7
        pick = (lax.broadcasted_iota(I32, (96, UNITS * 128), 0) == panel).astype(F32).astype(BF16)
        listed = bl_ref[:, 0, :]
        high = (listed >> 6).astype(F32).astype(BF16)
        low = (listed & 63).astype(F32).astype(BF16)
        is_frame = lax.broadcasted_iota(I32, (FRAMES, UNITS * 128), 0) == frame

        def taken(v):
            got = jnp.dot(v, pick, preferred_element_type=F32)
            return jnp.sum(jnp.where(is_frame, got, 0.0), axis=0, keepdims=True)

        block = (taken(high) * 64.0 + taken(low)).astype(I32)
        for i in range(32):
            table[i : i + 1, :] = om_ref[:, i * 128 : (i + 1) * 128]
        entry = table[...]
        in_row = (lax.broadcasted_iota(I32, (128, UNITS * 128), 0) == (block & 127)).astype(F32).astype(BF16)
        row_hit = lax.broadcasted_iota(I32, (32, UNITS * 128), 0) == (block >> 7)

        def looked(v):
            got = jnp.dot(v.astype(F32).astype(BF16), in_row, preferred_element_type=F32)
            return jnp.sum(jnp.where(row_hit, got, 0.0), axis=0, keepdims=True)

        found = (looked(entry >> 6) * 64.0 + looked(entry & 63)).astype(I32)
        for i in range(UNITS):
            pos[i : i + 1, :] = found[:, i * 128 : (i + 1) * 128]
        pall[mine] = pos[...]

    def make_targets():
        for k in range(2 * SIDE):
            at = pall[k]
            owner = at >> 7
            to_a = jnp.where(core == 0, owner >> 3, (owner >> 1) & 3)
            to_b = jnp.where(core == 0, (owner >> 1) & 3, owner >> 3)
            row = ((to_b * 2 + (owner & 1)) << 7) + (at & 127)
            row = jnp.where(to_a == a, row, -1)
            tgt[:, k * ENTRIES : (k + 1) * ENTRIES] = row[:, :ENTRIES]
            cut = 2 * PART
            early_tgt[:, k * cut : (k + 1) * cut] = row[:, :cut]
            late_tgt[:, k * PART : (k + 1) * PART] = row[:, cut:ENTRIES]

    def send_halo():
        for f in range(FRAMES):
            at = slice((f % 2) * 4, (f % 2) * 4 + 4)
            hs[0, f // 2, at, :] = px[f, 4 + ROWS : 8 + ROWS, :]
            hs[1, f // 2, at, :] = px[f, 8:12, :]
        halo_up.start()
        halo_down.start()

    def fill_halo():
        for f in range(FRAMES):
            top = hr[0, f // 2, (f % 2) * 4 : (f % 2) * 4 + 4, :]
            px[f, 4:8, :] = jnp.where(z > 0, top, 0.0)
            bottom = hr[1, f // 2, (f % 2) * 4 : (f % 2) * 4 + 4, :]
            px[f, 8 + ROWS : 12 + ROWS, :] = jnp.where(z < SIDE - 1, bottom, 0.0)

    def normalize(t):
        band = jnp.where(t < 4, t + 1, jnp.where(t == 4, 0, 5))
        row0 = pl.multiple_of(band * BAND, BAND)

        @pl.loop(0, FRAMES)
        def _(f):
            rows = px[f, pl.ds(row0, 2 * BAND), :]
            v = rows[4:28]
            mean = box_cols(box_rows(v)) * (1.0 / AREA)
            square = box_cols(box_rows(v * v)) * (1.0 / AREA)
            var = square - mean * mean
            scaled = (rows[8:24] - mean) * lax.rsqrt(var + EPSILON)
            kept = jnp.where(mk[f, pl.ds(row0, BAND), :] == 1, 0.0, scaled)
            for v in range(8):
                corr[v, pl.ds(pl.multiple_of(f * BAND, BAND), BAND), :] = kept[:, v * 128 : (v + 1) * 128]

        for r in range(4):
            for v in range(8):
                at = slice(r * COLS + v * 128, r * COLS + (v + 1) * 128)
                x_all[t, 0, :, at] = corr[v, pl.ds(r, PART, stride=4), :].astype(BF16)

    def z_start(t):
        for kind in range(2):
            z_direct(t, kind).start()

    def multiply(t, blocks=(0, 3), sets=None):
        low, high = blocks
        at = slice(low * PART, high * PART)
        left = x_all.at[t, low:high]
        for q in range(2):
            for own_half in range(2):
                h = core if own_half else 1 - core
                part = jnp.dot(
                    left[...].reshape((high - low) * PART, PIX), w4[h * 2 + q], preferred_element_type=F32
                ).astype(BF16)
                if own_half:
                    e_all[t, q, mine, at] = part
                else:
                    o_all[t, q, at] = part
            if sets:
                for c in entry_copies(sets[q][0], t, sets[q][1], q):
                    c.start()

    def send_entries(copies):
        for c in copies:
            c.start()

    def make_hits(t):
        row = tgt[pl.ds(t, 1), :]

        @pl.loop(0, SIDE)
        def _(blk):
            hit = (lax.broadcasted_iota(I32, (256, 2 * SIDE * ENTRIES), 0) + blk * 256) == row
            hits[blk] = hit.astype(F32).astype(BF16)

    def add_early():
        n = 4 * SIDE * PART
        row = early_tgt[pl.ds(end, 1), :]

        @pl.loop(0, SIDE)
        def _(blk):
            hit = (lax.broadcasted_iota(I32, (256, n), 0) + blk * 256) == row
            hits[blk, :, 0:n] = hit.astype(F32).astype(BF16)

        entries_arrived(end, end, EARLY)
        for q in range(2):
            terms = e_all[end, q, :, 0 : 2 * PART].reshape(n, QUART)
            sums = jnp.dot(hits[:, :, 0:n].reshape(SIDE * 256, n), terms, preferred_element_type=F32)
            acc2[q] += sums.reshape(SIDE, 256, QUART)

    def make_late_hits():
        row = late_tgt[pl.ds(end, 1), :]
        hit = lax.broadcasted_iota(I32, (SIDE * 256, 2 * SIDE * PART), 0) == row
        late_hits[...] = hit.astype(F32).astype(BF16)

    def add_late(q):
        terms = e_all[end, q, :, 2 * PART : ENTRIES].reshape(2 * SIDE * PART, QUART)
        sums = jnp.dot(late_hits[...], terms, preferred_element_type=F32)
        acc2[q] += sums.reshape(SIDE, 256, QUART)

    def add_unit(t, q):
        sums = jnp.dot(
            hits[...].reshape(SIDE * 256, 2 * SIDE * ENTRIES),
            e_all[t, q].reshape(2 * SIDE * ENTRIES, QUART),
            preferred_element_type=F32,
        )
        acc2[q] += sums.reshape(SIDE, 256, QUART)

    def add_all(t):
        make_hits(t)
        for q in range(2):
            entries_arrived(t, t, ALL, q)
            add_unit(t, q)

    loads[0].wait()
    loads[1].wait()
    normalize(0)
    pl.semaphore_wait(barrier, len(partners))
    z_start(0)
    loads[2].wait()
    loads[3].wait()
    for c in load_w:
        c.start()
    normalize(1)
    z_start(1)
    acc2[...] = jnp.zeros_like(acc2)
    send_halo()
    find_positions()
    for c in pos_copies:
        c.start()

    @pl.loop(2, STEPS)
    def _(t):
        @pl.when(t == 4)
        def _():
            halo_up.wait_recv()
            halo_down.wait_recv()
            fill_halo()

        normalize(t)
        z_start(t)

    @pl.loop(0, STEPS)
    def _(t):
        for kind in range(2):
            z_direct(t, kind).wait_recv()

        @pl.when(t < STEPS - 1)
        def _():
            for kind in range(2):
                z_forward(t, kind).start()

        @pl.when(t == 0)
        def _():
            for c in load_w:
                c.wait()

        multiply(t, sets=[(t, ALL)] * 2)

        @pl.when(t == 1)
        def _():
            for k in others():
                remote(pos, pall.at[k], ps_sem.at[0], pr_sem.at[k], sib).wait_recv()
            make_targets()

        @pl.when(t >= 1)
        def _():
            add_all(t - 1)


    def far(u, low, high):
        for i in range(low, high):
            for kind in range(2):
                z_forward((u - STEPS) * 3 + i, kind).wait_recv()

    far(end - 1, 0, 3)
    multiply(end - 1, sets=[(end - 1, ALL)] * 2)
    for kind in range(2):
        z_forward(STEPS - 3, kind).wait_send()
        z_forward(STEPS - 1, kind).start()
    add_all(end - 2)
    far(end, 0, 2)
    multiply(end, (0, 2))
    send_entries(entry_copies(end, end, EARLY))
    far(end, 2, 3)
    multiply(end, (2, 3), [(end + 1, LATE)] * 2)
    add_all(end - 1)
    add_early()
    make_late_hits()

    for q in range(2):
        entries_arrived(end + 1, end, LATE, q)
        add_late(q)
        for p in (2 * q, 2 * q + 1):
            at = slice((p % 2) * OWN, (p % 2 + 1) * OWN)
            for i in (2, 1, 3):
                s2[p, i - 1] = acc2[q, (b + i) % SIDE, :, at].astype(BF16)
                b_copy(i, p).start()
    for p in range(4):
        for i in range(1, SIDE):
            b_copy(i, p).wait_recv()
        at = slice((p % 2) * OWN, (p % 2 + 1) * OWN)
        total = acc2[p // 2, b, :, at] + (r2[p, 0].astype(F32) + r2[p, 1].astype(F32) + r2[p, 2].astype(F32))
        tot[p] = total
        for cc in range(2):
            fsum[p, cc] = total[cc * OWN : (cc + 1) * OWN, :].astype(BF16)
        for c in last_copies(p):
            c.start()
        own[core, p] = tot[p, pl.ds(pl.multiple_of(core * OWN, OWN), OWN), :]
    pick = (lax.broadcasted_iota(I32, (OWN, OWN), 0) == mp_ref[...]).astype(F32).astype(BF16)
    flip = (
        lax.broadcasted_iota(I32, (OWN, OWN), 0) + lax.broadcasted_iota(I32, (OWN, OWN), 1) == OWN - 1
    ).astype(F32).astype(BF16)
    for p in range(4):
        remote(own.at[0, p], own.at[0, p], fs_sem.at[p, 2], fr_sem.at[p, 2], sib).wait_recv()
        for h in range(2):
            ref = mir_in.at[h, p]
            remote(ref, ref, fs_sem.at[p, 0], fr_sem.at[p, h], dev(x, y, 0, z_far)).wait_recv()
        for h in range(2):
            rows = lax.dot_general(
                pick, mir_in[1 - h, p], (((0,), (0,)), ((), ())), preferred_element_type=F32
            ).astype(BF16)
            at = h * HALF + (3 - p) * OWN
            out_ref[0, :, at : at + OWN] = jnp.dot(rows, flip, preferred_element_type=F32)
    for p in range(4):
        for h in range(2):
            at = slice(h * HALF + p * OWN, h * HALF + (p + 1) * OWN)
            out_ref[0, :, at] = 0.5 * (own[h, p] + out_ref[0, :, at])

    halo_up.wait_send()
    halo_down.wait_send()
    for c in pos_copies:
        c.wait_send()

    @pl.loop(0, STEPS)
    def _(t):
        for kind in range(2):
            z_direct(t, kind).wait_send()

        @pl.when(t != STEPS - 3)
        def _():
            for kind in range(2):
                z_forward(t, kind).wait_send()

    @pl.loop(0, end)
    def _(t):
        for q in range(2):
            for c in entry_copies(t, t, ALL, q):
                c.wait_send()

    for c in entry_copies(end, end, EARLY):
        c.wait_send()
    for q in range(2):
        for c in entry_copies(end + 1, end, LATE, q):
            c.wait_send()

    for p in range(4):
        for i in range(1, SIDE):
            b_copy(i, p).wait_send()
        for c in last_copies(p):
            c.wait_send()


def shards(frame_pixels, bragg_mask, interp, block_list, owner_map, mirror_pair):
    vmem = pl.BlockSpec(memory_space=pltpu.VMEM)
    hbm = pl.BlockSpec(memory_space=pl.ANY)
    dma = pltpu.SemaphoreType.DMA
    return pl.pallas_call(
        kernel,
        out_shape=jax.ShapeDtypeStruct((1, OWN, VOX), F32),
        in_specs=[hbm, hbm, hbm, vmem, vmem, vmem],
        out_specs=vmem,
        scratch_shapes=[
            pltpu.VMEM((FRAMES, ROWS + 16, COLS), F32),
            pltpu.VMEM((FRAMES, ROWS, COLS), I32),
            pltpu.VMEM((4, PIX, QUART), BF16),
            pltpu.VMEM((8, FRAMES * BAND, 128), F32),
            pltpu.VMEM((UNITS, 3, PART, PIX), BF16),
            pltpu.VMEM((ENTRIES, QUART), F32),
            pltpu.VMEM((UNITS, 2, ENTRIES, QUART), BF16),
            pltpu.VMEM((UNITS, 2, 2 * SIDE, ENTRIES, QUART), BF16),
            pltpu.VMEM((2, SIDE, 256, QUART), F32),
            pltpu.VMEM((SIDE, 256, 2 * SIDE * ENTRIES), BF16),
            pltpu.VMEM((32, 128), I32),
            pltpu.VMEM((8, 128), I32),
            pltpu.VMEM((2 * SIDE, 8, 128), I32),
            pltpu.VMEM((8, 2 * SIDE * ENTRIES), I32),
            pltpu.VMEM((8, 4 * SIDE * PART), I32),
            pltpu.VMEM((8, 2 * SIDE * PART), I32),
            pltpu.VMEM((SIDE * 256, 2 * SIDE * PART), BF16),
            pltpu.VMEM((2, FRAMES // 2, 8, COLS), F32),
            pltpu.VMEM((2, FRAMES // 2, 8, COLS), F32),
            pltpu.VMEM((4, 3, 256, OWN), BF16),
            pltpu.VMEM((4, 3, 256, OWN), BF16),
            pltpu.VMEM((4, 2, OWN, OWN), BF16),
            pltpu.VMEM((4, 256, OWN), F32),
            pltpu.VMEM((2, 4, OWN, OWN), BF16),
            pltpu.VMEM((2, 4, OWN, OWN), F32),
            dma((4,)),
            dma((4,)),
            dma((2,)),
            dma((2,)),
            dma((7,)),
            dma((8,)),
            dma((STEPS, 4)),
            dma((STEPS, 4)),
            dma((UNITS + 1, 2, 7)),
            dma((UNITS + 1, 2, 8)),
            dma((4, 3)),
            dma((4, 3)),
            dma((4, 3)),
            dma((4, 3)),
        ],
        compiler_params=pltpu.CompilerParams(
            collective_id=0, has_side_effects=True, vmem_limit_bytes=60 * 1024 * 1024
        ),
    )(frame_pixels, bragg_mask, interp, block_list, owner_map, mirror_pair)


def solution(mesh):
    return jax.shard_map(
        shards,
        mesh=mesh,
        in_specs=(
            P("frames", "slabs", None),
            P("frames", "slabs", None),
            P("slabs", None, None),
            P("frames", "slabs", None),
            P("slabs", None),
            P("slabs", None),
        ),
        out_specs=P("slabs", "frames", None),
        check_vma=False,
    )
```

```python
import jax
import jax.numpy as jnp
from jax import lax
from jax.experimental import pallas as pl
from jax.experimental.pallas import tpu as pltpu
from jax.sharding import PartitionSpec as P

MESH = pl.DeviceIdType.MESH
F32 = jnp.float32
BF16 = jnp.bfloat16
I32 = jnp.int32

EPSILON = 1e-05
AREA = 81
SIDE = 4
FRAMES = 8
ROWS = 96
COLS = 1024
VOX = 1024
HALF = 512
QUART = 256
FIRST_ROWS = 40
PIX = 4096
BAND = 16
STEPS = ROWS // BAND
PART = FRAMES * BAND // 4
ENTRIES = 3 * PART
UNITS = STEPS + STEPS // 3
OWN = 128
ALL = pl.ds(0, ENTRIES)
EARLY = pl.ds(0, 2 * PART)
LATE = pl.ds(2 * PART, PART)


def spread(v, amount, axis):
    return pltpu.roll(v, amount % v.shape[axis], axis)


def box_rows(v):
    n = v.shape[0] - 8
    s2 = v[0 : n + 7] + v[1 : n + 8]
    s4 = s2[0 : n + 5] + s2[2 : n + 7]
    s8 = s4[0:n] + s4[4 : n + 4]
    return s8 + v[8 : n + 8]


def box_cols(h):
    h = jnp.concatenate([h, jnp.zeros((h.shape[0], 128), F32)], axis=1)
    s2 = h + spread(h, -1, 1)
    s4 = s2 + spread(s2, -2, 1)
    total = s4 + spread(s4, 4, 1) + spread(h, -4, 1)
    return total[:, :COLS]


def kernel(
    px_hbm, mk_hbm, w_hbm, bl_ref, om_ref, mp_ref, out_ref,
    px, mk, w4, corr, x_all, acc, o_all, e_all, acc2, hits, table, pos, pall, tgt, early_tgt, late_tgt, late_hits,
    hs, hr, s2, r2, fsum, tot, mir_in, own,
    ld_sem, lw_sem, hs_sem, hr_sem, ps_sem, pr_sem, zs_sem, zr_sem,
    as_sem, ar_sem, bs_sem, br_sem, fs_sem, fr_sem,
):
    me = lax.axis_index("frames")
    z = lax.axis_index("slabs")
    core = me % 2
    y = (me // 2) % SIDE
    x = me // (2 * SIDE)
    a = jnp.where(core == 0, x, y)
    b = jnp.where(core == 0, y, x)
    mine = a * 2 + core

    def dev(xx, yy, cc, zz):
        return {"frames": (xx * SIDE + yy) * 2 + cc, "slabs": zz}

    def along_b(i):
        bb = (b + i) % SIDE
        return dev(jnp.where(core == 0, x, bb), jnp.where(core == 0, bb, y), core, z)

    z_up = (z + 1) % SIDE
    z_down = (z + SIDE - 1) % SIDE
    z_far = (z + 2) % SIDE
    up = dev(x, y, core, z_up)
    down = dev(x, y, core, z_down)
    sib = dev(x, y, 1 - core, z)

    def along_a(i):
        aa = (a + i) % SIDE
        return dev(jnp.where(core == 0, aa, x), jnp.where(core == 0, y, aa), core, z)

    def along_other(i):
        aa = (b + i) % SIDE
        return dev(jnp.where(core == 0, x, aa), jnp.where(core == 0, aa, y), 1 - core, z)

    def remote(src, dst, ssem, rsem, to):
        return pltpu.make_async_remote_copy(
            src_ref=src, dst_ref=dst, send_sem=ssem, recv_sem=rsem, device_id=to, device_id_type=MESH
        )

    first = FIRST_ROWS
    loads = [
        pltpu.make_async_copy(px_hbm.at[:, pl.ds(0, first), :], px.at[:, pl.ds(8, first), :], ld_sem.at[0]),
        pltpu.make_async_copy(mk_hbm.at[:, pl.ds(0, first), :], mk.at[:, pl.ds(0, first), :], ld_sem.at[1]),
        pltpu.make_async_copy(
            px_hbm.at[:, pl.ds(first, ROWS - first), :], px.at[:, pl.ds(8 + first, ROWS - first), :], ld_sem.at[2]
        ),
        pltpu.make_async_copy(
            mk_hbm.at[:, pl.ds(first, ROWS - first), :], mk.at[:, pl.ds(first, ROWS - first), :], ld_sem.at[3]
        ),
    ]
    load_w = [
        pltpu.make_async_copy(w_hbm.at[0, :, pl.ds(i * QUART, QUART)], w4.at[i], lw_sem.at[i]) for i in range(4)
    ]
    for c in loads:
        c.start()

    barrier = pltpu.get_barrier_semaphore()
    partners = [up, down, sib, dev(x, y, core, z_far), dev(x, y, 1 - core, z_far)]
    for i in range(1, SIDE):
        for cc in range(2):
            partners.append(dev((x + i) % SIDE, y, cc, z))
            partners.append(dev(x, (y + i) % SIDE, cc, z))
    for to in partners:
        pl.semaphore_signal(barrier, inc=1, device_id=to, device_id_type=MESH)

    halo_up = remote(hs.at[0], hr.at[0], hs_sem.at[0], hr_sem.at[0], up)
    halo_down = remote(hs.at[1], hr.at[1], hs_sem.at[1], hr_sem.at[1], down)

    end = UNITS - 1

    def z_direct(t, kind):
        return remote(x_all.at[t, 0], x_all.at[t, 1 + kind], zs_sem.at[t, kind], zr_sem.at[t, kind], (up, down)[kind])

    def z_forward(t, kind):
        at = pl.ds(kind * (PIX // 2), PIX // 2)
        src, dst = x_all.at[t, 1 + kind, :, at], x_all.at[STEPS + t // 3, t % 3, :, at]
        return remote(src, dst, zs_sem.at[t, 2 + kind], zr_sem.at[t, 2 + kind], (up, down)[kind])

    def entry_copies(n, t, at, q=None):
        cols, m = (pl.ds(0, 2), 0) if q is None else (pl.ds(q, 1), q)
        slot = b * 2 + core
        copies = []
        for i in range(SIDE):
            src, dst = o_all.at[t, cols, at], e_all.at[t, cols, slot, at]
            copies.append(remote(src, dst, as_sem.at[n, m, i], ar_sem.at[n, m, slot], along_other(i)))
        for i in range(1, SIDE):
            ref = e_all.at[t, cols, mine, at]
            copies.append(remote(ref, ref, as_sem.at[n, m, 3 + i], ar_sem.at[n, m, mine], along_a(i)))
        return copies

    def others():
        return [a * 2 + 1 - core] + [((a + i) % SIDE) * 2 + g for i in range(1, SIDE) for g in range(2)]

    def entries_arrived(n, t, at, q=None):
        cols, m = (pl.ds(0, 2), 0) if q is None else (pl.ds(q, 1), q)
        for k in others():
            ref = e_all.at[t, cols, k, at]
            remote(ref, ref, as_sem.at[n, m, 0], ar_sem.at[n, m, k], sib).wait_recv()

    def b_copy(i, q):
        return remote(s2.at[q, i - 1], r2.at[q, i - 1], bs_sem.at[q, i - 1], br_sem.at[q, i - 1], along_b(i))

    def last_copies(q):
        ref = tot.at[q, pl.ds(pl.multiple_of((1 - core) * OWN, OWN), OWN)]
        return [
            remote(fsum.at[q, 0], mir_in.at[core, q], fs_sem.at[q, 0], fr_sem.at[q, core], dev(x, y, 0, z_far)),
            remote(fsum.at[q, 1], mir_in.at[core, q], fs_sem.at[q, 1], fr_sem.at[q, core], dev(x, y, 1, z_far)),
            remote(ref, own.at[core, q], fs_sem.at[q, 2], fr_sem.at[q, 2], sib),
        ]

    pos_copies = []
    for i in range(SIDE):
        slot = b * 2 + core
        pos_copies.append(remote(pos, pall.at[slot], ps_sem.at[i], pr_sem.at[slot], along_other(i)))
    for i in range(1, SIDE):
        pos_copies.append(remote(pos, pall.at[mine], ps_sem.at[3 + i], pr_sem.at[mine], along_a(i)))

    def find_positions():
        lane = lax.broadcasted_iota(I32, (1, UNITS * 128), 1)
        unit = lane >> 7
        third = (lane >> 5) & 3
        near = unit < STEPS
        step = jnp.where(near, unit, (unit - STEPS) * 3 + third)
        band = jnp.where(step < 4, step + 1, jnp.where(step == 4, 0, 5))
        apart = jnp.where(near, jnp.where(third == 0, 0, jnp.where(third == 1, 3, 1)), 2)
        panel = ((z + apart) & 3) * 24 + band * 4 + (lane & 3)
        frame = (lane >> 2) & 7
        pick = (lax.broadcasted_iota(I32, (96, UNITS * 128), 0) == panel).astype(F32).astype(BF16)
        listed = bl_ref[:, 0, :]
        high = (listed >> 6).astype(F32).astype(BF16)
        low = (listed & 63).astype(F32).astype(BF16)
        is_frame = lax.broadcasted_iota(I32, (FRAMES, UNITS * 128), 0) == frame

        def taken(v):
            got = jnp.dot(v, pick, preferred_element_type=F32)
            return jnp.sum(jnp.where(is_frame, got, 0.0), axis=0, keepdims=True)

        block = (taken(high) * 64.0 + taken(low)).astype(I32)
        for i in range(32):
            table[i : i + 1, :] = om_ref[:, i * 128 : (i + 1) * 128]
        entry = table[...]
        in_row = (lax.broadcasted_iota(I32, (128, UNITS * 128), 0) == (block & 127)).astype(F32).astype(BF16)
        row_hit = lax.broadcasted_iota(I32, (32, UNITS * 128), 0) == (block >> 7)

        def looked(v):
            got = jnp.dot(v.astype(F32).astype(BF16), in_row, preferred_element_type=F32)
            return jnp.sum(jnp.where(row_hit, got, 0.0), axis=0, keepdims=True)

        found = (looked(entry >> 6) * 64.0 + looked(entry & 63)).astype(I32)
        for i in range(UNITS):
            pos[i : i + 1, :] = found[:, i * 128 : (i + 1) * 128]
        pall[mine] = pos[...]

    def make_targets():
        for k in range(2 * SIDE):
            at = pall[k]
            owner = at >> 7
            to_a = jnp.where(core == 0, owner >> 3, (owner >> 1) & 3)
            to_b = jnp.where(core == 0, (owner >> 1) & 3, owner >> 3)
            row = ((to_b * 2 + (owner & 1)) << 7) + (at & 127)
            row = jnp.where(to_a == a, row, -1)
            tgt[:, k * ENTRIES : (k + 1) * ENTRIES] = row[:, :ENTRIES]
            cut = 2 * PART
            early_tgt[:, k * cut : (k + 1) * cut] = row[:, :cut]
            late_tgt[:, k * PART : (k + 1) * PART] = row[:, cut:ENTRIES]

    def send_halo():
        for f in range(FRAMES):
            at = slice((f % 2) * 4, (f % 2) * 4 + 4)
            hs[0, f // 2, at, :] = px[f, 4 + ROWS : 8 + ROWS, :]
            hs[1, f // 2, at, :] = px[f, 8:12, :]
        halo_up.start()
        halo_down.start()

    def fill_halo():
        for f in range(FRAMES):
            top = hr[0, f // 2, (f % 2) * 4 : (f % 2) * 4 + 4, :]
            px[f, 4:8, :] = jnp.where(z > 0, top, 0.0)
            bottom = hr[1, f // 2, (f % 2) * 4 : (f % 2) * 4 + 4, :]
            px[f, 8 + ROWS : 12 + ROWS, :] = jnp.where(z < SIDE - 1, bottom, 0.0)

    def normalize(t):
        band = jnp.where(t < 4, t + 1, jnp.where(t == 4, 0, 5))
        row0 = pl.multiple_of(band * BAND, BAND)

        @pl.loop(0, FRAMES)
        def _(f):
            rows = px[f, pl.ds(row0, 2 * BAND), :]
            v = rows[4:28]
            mean = box_cols(box_rows(v)) * (1.0 / AREA)
            square = box_cols(box_rows(v * v)) * (1.0 / AREA)
            var = square - mean * mean
            scaled = (rows[8:24] - mean) * lax.rsqrt(var + EPSILON)
            kept = jnp.where(mk[f, pl.ds(row0, BAND), :] == 1, 0.0, scaled)
            for v in range(8):
                corr[v, pl.ds(pl.multiple_of(f * BAND, BAND), BAND), :] = kept[:, v * 128 : (v + 1) * 128]

        for r in range(4):
            for v in range(8):
                at = slice(r * COLS + v * 128, r * COLS + (v + 1) * 128)
                x_all[t, 0, :, at] = corr[v, pl.ds(r, PART, stride=4), :].astype(BF16)

    def z_start(t):
        for kind in range(2):
            z_direct(t, kind).start()

    def multiply(t, blocks=(0, 3), sets=None):
        low, high = blocks
        at = slice(low * PART, high * PART)
        left = x_all.at[t, low:high]
        for q in range(2):
            for own_half in range(2):
                h = core if own_half else 1 - core
                part = jnp.dot(
                    left[...].reshape((high - low) * PART, PIX), w4[h * 2 + q], preferred_element_type=F32
                ).astype(BF16)
                if own_half:
                    e_all[t, q, mine, at] = part
                else:
                    o_all[t, q, at] = part
                if sets:
                    copies = entry_copies(sets[q][0], t, sets[q][1], q)
                    for i in (5, 4, 6) if own_half else (2, 1, 3, 0):
                        copies[i].start()

    def send_entries(copies):
        for c in copies:
            c.start()

    def make_hits(t):
        row = tgt[pl.ds(t, 1), :]

        @pl.loop(0, SIDE)
        def _(blk):
            hit = (lax.broadcasted_iota(I32, (256, 2 * SIDE * ENTRIES), 0) + blk * 256) == row
            hits[blk] = hit.astype(F32).astype(BF16)

    def add_early():
        n = 4 * SIDE * PART
        row = early_tgt[pl.ds(end, 1), :]

        @pl.loop(0, SIDE)
        def _(blk):
            hit = (lax.broadcasted_iota(I32, (256, n), 0) + blk * 256) == row
            hits[blk, :, 0:n] = hit.astype(F32).astype(BF16)

        entries_arrived(end, end, EARLY)
        for q in range(2):
            terms = e_all[end, q, :, 0 : 2 * PART].reshape(n, QUART)
            sums = jnp.dot(hits[:, :, 0:n].reshape(SIDE * 256, n), terms, preferred_element_type=F32)
            acc2[q] += sums.reshape(SIDE, 256, QUART)

    def make_late_hits():
        row = late_tgt[pl.ds(end, 1), :]
        hit = lax.broadcasted_iota(I32, (SIDE * 256, 2 * SIDE * PART), 0) == row
        late_hits[...] = hit.astype(F32).astype(BF16)

    def add_late(q):
        terms = e_all[end, q, :, 2 * PART : ENTRIES].reshape(2 * SIDE * PART, QUART)
        sums = jnp.dot(late_hits[...], terms, preferred_element_type=F32)
        acc2[q] += sums.reshape(SIDE, 256, QUART)

    def add_unit(t, q):
        sums = jnp.dot(
            hits[...].reshape(SIDE * 256, 2 * SIDE * ENTRIES),
            e_all[t, q].reshape(2 * SIDE * ENTRIES, QUART),
            preferred_element_type=F32,
        )
        acc2[q] += sums.reshape(SIDE, 256, QUART)

    def add_all(t):
        make_hits(t)
        for q in range(2):
            entries_arrived(t, t, ALL, q)
            add_unit(t, q)

    loads[0].wait()
    loads[1].wait()
    normalize(0)
    pl.semaphore_wait(barrier, len(partners))
    z_start(0)
    loads[2].wait()
    loads[3].wait()
    for c in load_w:
        c.start()
    normalize(1)
    z_start(1)
    acc2[...] = jnp.zeros_like(acc2)
    send_halo()
    find_positions()
    for c in pos_copies:
        c.start()

    @pl.loop(2, STEPS)
    def _(t):
        @pl.when(t == 4)
        def _():
            halo_up.wait_recv()
            halo_down.wait_recv()
            fill_halo()

        normalize(t)
        z_start(t)

    @pl.loop(0, STEPS)
    def _(t):
        for kind in range(2):
            z_direct(t, kind).wait_recv()

        @pl.when(t < STEPS - 1)
        def _():
            for kind in range(2):
                z_forward(t, kind).start()

        @pl.when(t == 0)
        def _():
            for c in load_w:
                c.wait()

        multiply(t, sets=[(t, ALL)] * 2)

        @pl.when(t == 1)
        def _():
            for k in others():
                remote(pos, pall.at[k], ps_sem.at[0], pr_sem.at[k], sib).wait_recv()
            make_targets()

        @pl.when(t >= 1)
        def _():
            add_all(t - 1)


    def far(u, low, high):
        for i in range(low, high):
            for kind in range(2):
                z_forward((u - STEPS) * 3 + i, kind).wait_recv()

    far(end - 1, 0, 3)
    multiply(end - 1, sets=[(end - 1, ALL)] * 2)
    for kind in range(2):
        z_forward(STEPS - 3, kind).wait_send()
        z_forward(STEPS - 1, kind).start()
    add_all(end - 2)
    far(end, 0, 2)
    multiply(end, (0, 2))
    send_entries(entry_copies(end, end, EARLY))
    far(end, 2, 3)
    multiply(end, (2, 3), [(end + 1, LATE)] * 2)
    add_all(end - 1)
    add_early()
    make_late_hits()

    for q in range(2):
        entries_arrived(end + 1, end, LATE, q)
        add_late(q)
        for p in (2 * q, 2 * q + 1):
            at = slice((p % 2) * OWN, (p % 2 + 1) * OWN)
            for i in (2, 1, 3):
                s2[p, i - 1] = acc2[q, (b + i) % SIDE, :, at].astype(BF16)
                b_copy(i, p).start()
    for p in range(4):
        for i in range(1, SIDE):
            b_copy(i, p).wait_recv()
        at = slice((p % 2) * OWN, (p % 2 + 1) * OWN)
        total = acc2[p // 2, b, :, at] + (r2[p, 0].astype(F32) + r2[p, 1].astype(F32) + r2[p, 2].astype(F32))
        tot[p] = total
        for cc in range(2):
            fsum[p, cc] = total[cc * OWN : (cc + 1) * OWN, :].astype(BF16)
        for c in last_copies(p):
            c.start()
        own[core, p] = tot[p, pl.ds(pl.multiple_of(core * OWN, OWN), OWN), :]
    pick = (lax.broadcasted_iota(I32, (OWN, OWN), 0) == mp_ref[...]).astype(F32).astype(BF16)
    flip = (
        lax.broadcasted_iota(I32, (OWN, OWN), 0) + lax.broadcasted_iota(I32, (OWN, OWN), 1) == OWN - 1
    ).astype(F32).astype(BF16)
    for p in range(4):
        remote(own.at[0, p], own.at[0, p], fs_sem.at[p, 2], fr_sem.at[p, 2], sib).wait_recv()
        for h in range(2):
            ref = mir_in.at[h, p]
            remote(ref, ref, fs_sem.at[p, 0], fr_sem.at[p, h], dev(x, y, 0, z_far)).wait_recv()
        for h in range(2):
            rows = lax.dot_general(
                pick, mir_in[1 - h, p], (((0,), (0,)), ((), ())), preferred_element_type=F32
            ).astype(BF16)
            at = h * HALF + (3 - p) * OWN
            out_ref[0, :, at : at + OWN] = jnp.dot(rows, flip, preferred_element_type=F32)
    for p in range(4):
        for h in range(2):
            at = slice(h * HALF + p * OWN, h * HALF + (p + 1) * OWN)
            out_ref[0, :, at] = 0.5 * (own[h, p] + out_ref[0, :, at])

    halo_up.wait_send()
    halo_down.wait_send()
    for c in pos_copies:
        c.wait_send()

    @pl.loop(0, STEPS)
    def _(t):
        for kind in range(2):
            z_direct(t, kind).wait_send()

        @pl.when(t != STEPS - 3)
        def _():
            for kind in range(2):
                z_forward(t, kind).wait_send()

    @pl.loop(0, end)
    def _(t):
        for q in range(2):
            for c in entry_copies(t, t, ALL, q):
                c.wait_send()

    for c in entry_copies(end, end, EARLY):
        c.wait_send()
    for q in range(2):
        for c in entry_copies(end + 1, end, LATE, q):
            c.wait_send()

    for p in range(4):
        for i in range(1, SIDE):
            b_copy(i, p).wait_send()
        for c in last_copies(p):
            c.wait_send()


def shards(frame_pixels, bragg_mask, interp, block_list, owner_map, mirror_pair):
    vmem = pl.BlockSpec(memory_space=pltpu.VMEM)
    hbm = pl.BlockSpec(memory_space=pl.ANY)
    dma = pltpu.SemaphoreType.DMA
    return pl.pallas_call(
        kernel,
        out_shape=jax.ShapeDtypeStruct((1, OWN, VOX), F32),
        in_specs=[hbm, hbm, hbm, vmem, vmem, vmem],
        out_specs=vmem,
        scratch_shapes=[
            pltpu.VMEM((FRAMES, ROWS + 16, COLS), F32),
            pltpu.VMEM((FRAMES, ROWS, COLS), I32),
            pltpu.VMEM((4, PIX, QUART), BF16),
            pltpu.VMEM((8, FRAMES * BAND, 128), F32),
            pltpu.VMEM((UNITS, 3, PART, PIX), BF16),
            pltpu.VMEM((ENTRIES, QUART), F32),
            pltpu.VMEM((UNITS, 2, ENTRIES, QUART), BF16),
            pltpu.VMEM((UNITS, 2, 2 * SIDE, ENTRIES, QUART), BF16),
            pltpu.VMEM((2, SIDE, 256, QUART), F32),
            pltpu.VMEM((SIDE, 256, 2 * SIDE * ENTRIES), BF16),
            pltpu.VMEM((32, 128), I32),
            pltpu.VMEM((8, 128), I32),
            pltpu.VMEM((2 * SIDE, 8, 128), I32),
            pltpu.VMEM((8, 2 * SIDE * ENTRIES), I32),
            pltpu.VMEM((8, 4 * SIDE * PART), I32),
            pltpu.VMEM((8, 2 * SIDE * PART), I32),
            pltpu.VMEM((SIDE * 256, 2 * SIDE * PART), BF16),
            pltpu.VMEM((2, FRAMES // 2, 8, COLS), F32),
            pltpu.VMEM((2, FRAMES // 2, 8, COLS), F32),
            pltpu.VMEM((4, 3, 256, OWN), BF16),
            pltpu.VMEM((4, 3, 256, OWN), BF16),
            pltpu.VMEM((4, 2, OWN, OWN), BF16),
            pltpu.VMEM((4, 256, OWN), F32),
            pltpu.VMEM((2, 4, OWN, OWN), BF16),
            pltpu.VMEM((2, 4, OWN, OWN), F32),
            dma((4,)),
            dma((4,)),
            dma((2,)),
            dma((2,)),
            dma((7,)),
            dma((8,)),
            dma((STEPS, 4)),
            dma((STEPS, 4)),
            dma((UNITS + 1, 2, 7)),
            dma((UNITS + 1, 2, 8)),
            dma((4, 3)),
            dma((4, 3)),
            dma((4, 3)),
            dma((4, 3)),
        ],
        compiler_params=pltpu.CompilerParams(
            collective_id=0, has_side_effects=True, vmem_limit_bytes=60 * 1024 * 1024
        ),
    )(frame_pixels, bragg_mask, interp, block_list, owner_map, mirror_pair)


def solution(mesh):
    return jax.shard_map(
        shards,
        mesh=mesh,
        in_specs=(
            P("frames", "slabs", None),
            P("frames", "slabs", None),
            P("slabs", None, None),
            P("frames", "slabs", None),
            P("slabs", None),
            P("slabs", None),
        ),
        out_specs=P("slabs", "frames", None),
        check_vma=False,
    )
```

```python
import jax
import jax.numpy as jnp
from jax import lax
from jax.experimental import pallas as pl
from jax.experimental.pallas import tpu as pltpu
from jax.sharding import PartitionSpec as P

MESH = pl.DeviceIdType.MESH
F32 = jnp.float32
BF16 = jnp.bfloat16
I32 = jnp.int32

EPSILON = 1e-05
AREA = 81
SIDE = 4
FRAMES = 8
ROWS = 96
COLS = 1024
VOX = 1024
HALF = 512
QUART = 256
FIRST_ROWS = 40
PIX = 4096
BAND = 16
STEPS = ROWS // BAND
PART = FRAMES * BAND // 4
ENTRIES = 3 * PART
UNITS = STEPS + STEPS // 3
OWN = 128
ALL = pl.ds(0, ENTRIES)
EARLY = pl.ds(0, 2 * PART)
LATE = pl.ds(2 * PART, PART)


def spread(v, amount, axis):
    return pltpu.roll(v, amount % v.shape[axis], axis)


def box_rows(v):
    n = v.shape[0] - 8
    s2 = v[0 : n + 7] + v[1 : n + 8]
    s4 = s2[0 : n + 5] + s2[2 : n + 7]
    s8 = s4[0:n] + s4[4 : n + 4]
    return s8 + v[8 : n + 8]


def box_cols(h):
    h = jnp.concatenate([h, jnp.zeros((h.shape[0], 128), F32)], axis=1)
    s2 = h + spread(h, -1, 1)
    s4 = s2 + spread(s2, -2, 1)
    total = s4 + spread(s4, 4, 1) + spread(h, -4, 1)
    return total[:, :COLS]


def kernel(
    px_hbm, mk_hbm, w_hbm, bl_ref, om_ref, mp_ref, out_ref,
    px, mk, w4, corr, x_all, acc, o_all, e_all, acc2, hits, table, pos, pall, tgt, early_tgt, late_tgt, late_hits,
    hs, hr, s2, r2, fsum, tot, mir_in, own,
    ld_sem, lw_sem, hs_sem, hr_sem, ps_sem, pr_sem, zs_sem, zr_sem,
    as_sem, ar_sem, bs_sem, br_sem, fs_sem, fr_sem,
):
    me = lax.axis_index("frames")
    z = lax.axis_index("slabs")
    core = me % 2
    y = (me // 2) % SIDE
    x = me // (2 * SIDE)
    a = jnp.where(core == 0, x, y)
    b = jnp.where(core == 0, y, x)
    mine = a * 2 + core

    def dev(xx, yy, cc, zz):
        return {"frames": (xx * SIDE + yy) * 2 + cc, "slabs": zz}

    def along_b(i):
        bb = (b + i) % SIDE
        return dev(jnp.where(core == 0, x, bb), jnp.where(core == 0, bb, y), core, z)

    z_up = (z + 1) % SIDE
    z_down = (z + SIDE - 1) % SIDE
    z_far = (z + 2) % SIDE
    up = dev(x, y, core, z_up)
    down = dev(x, y, core, z_down)
    sib = dev(x, y, 1 - core, z)

    def along_a(i):
        aa = (a + i) % SIDE
        return dev(jnp.where(core == 0, aa, x), jnp.where(core == 0, y, aa), core, z)

    def along_other(i):
        aa = (b + i) % SIDE
        return dev(jnp.where(core == 0, x, aa), jnp.where(core == 0, aa, y), 1 - core, z)

    def remote(src, dst, ssem, rsem, to):
        return pltpu.make_async_remote_copy(
            src_ref=src, dst_ref=dst, send_sem=ssem, recv_sem=rsem, device_id=to, device_id_type=MESH
        )

    first = FIRST_ROWS
    loads = [
        pltpu.make_async_copy(px_hbm.at[:, pl.ds(0, first), :], px.at[:, pl.ds(8, first), :], ld_sem.at[0]),
        pltpu.make_async_copy(mk_hbm.at[:, pl.ds(0, first), :], mk.at[:, pl.ds(0, first), :], ld_sem.at[1]),
        pltpu.make_async_copy(
            px_hbm.at[:, pl.ds(first, ROWS - first), :], px.at[:, pl.ds(8 + first, ROWS - first), :], ld_sem.at[2]
        ),
        pltpu.make_async_copy(
            mk_hbm.at[:, pl.ds(first, ROWS - first), :], mk.at[:, pl.ds(first, ROWS - first), :], ld_sem.at[3]
        ),
    ]
    load_w = [
        pltpu.make_async_copy(w_hbm.at[0, :, pl.ds(i * QUART, QUART)], w4.at[i], lw_sem.at[i]) for i in range(4)
    ]
    for c in loads:
        c.start()

    barrier = pltpu.get_barrier_semaphore()
    partners = [up, down, sib, dev(x, y, core, z_far), dev(x, y, 1 - core, z_far)]
    for i in range(1, SIDE):
        for cc in range(2):
            partners.append(dev((x + i) % SIDE, y, cc, z))
            partners.append(dev(x, (y + i) % SIDE, cc, z))
    for to in partners:
        pl.semaphore_signal(barrier, inc=1, device_id=to, device_id_type=MESH)

    halo_up = remote(hs.at[0], hr.at[0], hs_sem.at[0], hr_sem.at[0], up)
    halo_down = remote(hs.at[1], hr.at[1], hs_sem.at[1], hr_sem.at[1], down)

    end = UNITS - 1

    def z_direct(t, kind):
        return remote(x_all.at[t, 0], x_all.at[t, 1 + kind], zs_sem.at[t, kind], zr_sem.at[t, kind], (up, down)[kind])

    def z_forward(t, kind):
        at = pl.ds(kind * (PIX // 2), PIX // 2)
        src, dst = x_all.at[t, 1 + kind, :, at], x_all.at[STEPS + t // 3, t % 3, :, at]
        return remote(src, dst, zs_sem.at[t, 2 + kind], zr_sem.at[t, 2 + kind], (up, down)[kind])

    def entry_copies(n, t, at, q=None):
        cols, m = (pl.ds(0, 2), 0) if q is None else (pl.ds(q, 1), q)
        slot = b * 2 + core
        copies = []
        for i in range(SIDE):
            src, dst = o_all.at[t, cols, at], e_all.at[t, cols, slot, at]
            copies.append(remote(src, dst, as_sem.at[n, m, i], ar_sem.at[n, m, slot], along_other(i)))
        for i in range(1, SIDE):
            ref = e_all.at[t, cols, mine, at]
            copies.append(remote(ref, ref, as_sem.at[n, m, 3 + i], ar_sem.at[n, m, mine], along_a(i)))
        return copies

    def others():
        return [a * 2 + 1 - core] + [((a + i) % SIDE) * 2 + g for i in range(1, SIDE) for g in range(2)]

    def entries_arrived(n, t, at, q=None):
        cols, m = (pl.ds(0, 2), 0) if q is None else (pl.ds(q, 1), q)
        for k in others():
            ref = e_all.at[t, cols, k, at]
            remote(ref, ref, as_sem.at[n, m, 0], ar_sem.at[n, m, k], sib).wait_recv()

    def b_copy(i, q):
        return remote(s2.at[q, i - 1], r2.at[q, i - 1], bs_sem.at[q, i - 1], br_sem.at[q, i - 1], along_b(i))

    def last_copies(q):
        ref = tot.at[q, pl.ds(pl.multiple_of((1 - core) * OWN, OWN), OWN)]
        return [
            remote(fsum.at[q, 0], mir_in.at[core, q], fs_sem.at[q, 0], fr_sem.at[q, core], dev(x, y, 0, z_far)),
            remote(fsum.at[q, 1], mir_in.at[core, q], fs_sem.at[q, 1], fr_sem.at[q, core], dev(x, y, 1, z_far)),
            remote(ref, own.at[core, q], fs_sem.at[q, 2], fr_sem.at[q, 2], sib),
        ]

    pos_copies = []
    for i in range(SIDE):
        slot = b * 2 + core
        pos_copies.append(remote(pos, pall.at[slot], ps_sem.at[i], pr_sem.at[slot], along_other(i)))
    for i in range(1, SIDE):
        pos_copies.append(remote(pos, pall.at[mine], ps_sem.at[3 + i], pr_sem.at[mine], along_a(i)))

    def find_positions():
        lane = lax.broadcasted_iota(I32, (1, UNITS * 128), 1)
        unit = lane >> 7
        third = (lane >> 5) & 3
        near = unit < STEPS
        step = jnp.where(near, unit, (unit - STEPS) * 3 + third)
        band = jnp.where(step < 4, step + 1, jnp.where(step == 4, 0, 5))
        apart = jnp.where(near, jnp.where(third == 0, 0, jnp.where(third == 1, 3, 1)), 2)
        panel = ((z + apart) & 3) * 24 + band * 4 + (lane & 3)
        frame = (lane >> 2) & 7
        pick = (lax.broadcasted_iota(I32, (96, UNITS * 128), 0) == panel).astype(F32).astype(BF16)
        listed = bl_ref[:, 0, :]
        high = (listed >> 6).astype(F32).astype(BF16)
        low = (listed & 63).astype(F32).astype(BF16)
        is_frame = lax.broadcasted_iota(I32, (FRAMES, UNITS * 128), 0) == frame

        def taken(v):
            got = jnp.dot(v, pick, preferred_element_type=F32)
            return jnp.sum(jnp.where(is_frame, got, 0.0), axis=0, keepdims=True)

        block = (taken(high) * 64.0 + taken(low)).astype(I32)
        for i in range(32):
            table[i : i + 1, :] = om_ref[:, i * 128 : (i + 1) * 128]
        entry = table[...]
        in_row = (lax.broadcasted_iota(I32, (128, UNITS * 128), 0) == (block & 127)).astype(F32).astype(BF16)
        row_hit = lax.broadcasted_iota(I32, (32, UNITS * 128), 0) == (block >> 7)

        def looked(v):
            got = jnp.dot(v.astype(F32).astype(BF16), in_row, preferred_element_type=F32)
            return jnp.sum(jnp.where(row_hit, got, 0.0), axis=0, keepdims=True)

        found = (looked(entry >> 6) * 64.0 + looked(entry & 63)).astype(I32)
        for i in range(UNITS):
            pos[i : i + 1, :] = found[:, i * 128 : (i + 1) * 128]
        pall[mine] = pos[...]

    def make_targets():
        for k in range(2 * SIDE):
            at = pall[k]
            owner = at >> 7
            to_a = jnp.where(core == 0, owner >> 3, (owner >> 1) & 3)
            to_b = jnp.where(core == 0, (owner >> 1) & 3, owner >> 3)
            row = ((to_b * 2 + (owner & 1)) << 7) + (at & 127)
            row = jnp.where(to_a == a, row, -1)
            tgt[:, k * ENTRIES : (k + 1) * ENTRIES] = row[:, :ENTRIES]
            cut = 2 * PART
            early_tgt[:, k * cut : (k + 1) * cut] = row[:, :cut]
            late_tgt[:, k * PART : (k + 1) * PART] = row[:, cut:ENTRIES]

    def send_halo():
        for f in range(FRAMES):
            at = slice((f % 2) * 4, (f % 2) * 4 + 4)
            hs[0, f // 2, at, :] = px[f, 4 + ROWS : 8 + ROWS, :]
            hs[1, f // 2, at, :] = px[f, 8:12, :]
        halo_up.start()
        halo_down.start()

    def fill_halo():
        for f in range(FRAMES):
            top = hr[0, f // 2, (f % 2) * 4 : (f % 2) * 4 + 4, :]
            px[f, 4:8, :] = jnp.where(z > 0, top, 0.0)
            bottom = hr[1, f // 2, (f % 2) * 4 : (f % 2) * 4 + 4, :]
            px[f, 8 + ROWS : 12 + ROWS, :] = jnp.where(z < SIDE - 1, bottom, 0.0)

    def normalize(t):
        band = jnp.where(t < 4, t + 1, jnp.where(t == 4, 0, 5))
        row0 = pl.multiple_of(band * BAND, BAND)

        @pl.loop(0, FRAMES)
        def _(f):
            rows = px[f, pl.ds(row0, 2 * BAND), :]
            v = rows[4:28]
            mean = box_cols(box_rows(v)) * (1.0 / AREA)
            square = box_cols(box_rows(v * v)) * (1.0 / AREA)
            var = square - mean * mean
            scaled = (rows[8:24] - mean) * lax.rsqrt(var + EPSILON)
            kept = jnp.where(mk[f, pl.ds(row0, BAND), :] == 1, 0.0, scaled)
            for v in range(8):
                corr[v, pl.ds(pl.multiple_of(f * BAND, BAND), BAND), :] = kept[:, v * 128 : (v + 1) * 128]

        for r in range(4):
            for v in range(8):
                at = slice(r * COLS + v * 128, r * COLS + (v + 1) * 128)
                x_all[t, 0, :, at] = corr[v, pl.ds(r, PART, stride=4), :].astype(BF16)

    def z_start(t):
        for kind in range(2):
            z_direct(t, kind).start()

    def multiply(t, blocks=(0, 3), sets=None):
        low, high = blocks
        at = slice(low * PART, high * PART)
        left = x_all.at[t, low:high]
        for q in range(2):
            for own_half in range(2):
                h = core if own_half else 1 - core
                part = jnp.dot(
                    left[...].reshape((high - low) * PART, PIX), w4[h * 2 + q], preferred_element_type=F32
                ).astype(BF16)
                if own_half:
                    e_all[t, q, mine, at] = part
                else:
                    o_all[t, q, at] = part
        if sets:
            for q in range(2):
                for c in entry_copies(sets[q][0], t, sets[q][1], q):
                    c.start()

    def send_entries(copies):
        for c in copies:
            c.start()

    def make_hits(t):
        row = tgt[pl.ds(t, 1), :]

        @pl.loop(0, SIDE)
        def _(blk):
            hit = (lax.broadcasted_iota(I32, (256, 2 * SIDE * ENTRIES), 0) + blk * 256) == row
            hits[blk] = hit.astype(F32).astype(BF16)

    def add_early():
        n = 4 * SIDE * PART
        row = early_tgt[pl.ds(end, 1), :]

        @pl.loop(0, SIDE)
        def _(blk):
            hit = (lax.broadcasted_iota(I32, (256, n), 0) + blk * 256) == row
            hits[blk, :, 0:n] = hit.astype(F32).astype(BF16)

        entries_arrived(end, end, EARLY)
        for q in range(2):
            terms = e_all[end, q, :, 0 : 2 * PART].reshape(n, QUART)
            sums = jnp.dot(hits[:, :, 0:n].reshape(SIDE * 256, n), terms, preferred_element_type=F32)
            acc2[q] += sums.reshape(SIDE, 256, QUART)

    def make_late_hits():
        row = late_tgt[pl.ds(end, 1), :]
        hit = lax.broadcasted_iota(I32, (SIDE * 256, 2 * SIDE * PART), 0) == row
        late_hits[...] = hit.astype(F32).astype(BF16)

    def add_late(q):
        terms = e_all[end, q, :, 2 * PART : ENTRIES].reshape(2 * SIDE * PART, QUART)
        sums = jnp.dot(late_hits[...], terms, preferred_element_type=F32)
        acc2[q] += sums.reshape(SIDE, 256, QUART)

    def add_unit(t, q):
        sums = jnp.dot(
            hits[...].reshape(SIDE * 256, 2 * SIDE * ENTRIES),
            e_all[t, q].reshape(2 * SIDE * ENTRIES, QUART),
            preferred_element_type=F32,
        )
        acc2[q] += sums.reshape(SIDE, 256, QUART)

    def add_all(t):
        make_hits(t)
        for q in range(2):
            entries_arrived(t, t, ALL, q)
            add_unit(t, q)

    loads[0].wait()
    loads[1].wait()
    normalize(0)
    pl.semaphore_wait(barrier, len(partners))
    z_start(0)
    loads[2].wait()
    loads[3].wait()
    for c in load_w:
        c.start()
    normalize(1)
    z_start(1)
    acc2[...] = jnp.zeros_like(acc2)
    send_halo()
    find_positions()
    for c in pos_copies:
        c.start()

    @pl.loop(2, STEPS)
    def _(t):
        @pl.when(t == 4)
        def _():
            halo_up.wait_recv()
            halo_down.wait_recv()
            fill_halo()

        normalize(t)
        z_start(t)

    @pl.loop(0, STEPS)
    def _(t):
        for kind in range(2):
            z_direct(t, kind).wait_recv()

        @pl.when(t < STEPS - 1)
        def _():
            for kind in range(2):
                z_forward(t, kind).start()

        @pl.when(t == 0)
        def _():
            for c in load_w:
                c.wait()

        multiply(t, sets=[(t, ALL)] * 2)

        @pl.when(t == 1)
        def _():
            for k in others():
                remote(pos, pall.at[k], ps_sem.at[0], pr_sem.at[k], sib).wait_recv()
            make_targets()

        @pl.when(t >= 1)
        def _():
            add_all(t - 1)


    def far(u, low, high):
        for i in range(low, high):
            for kind in range(2):
                z_forward((u - STEPS) * 3 + i, kind).wait_recv()

    far(end - 1, 0, 3)
    multiply(end - 1, sets=[(end - 1, ALL)] * 2)
    for kind in range(2):
        z_forward(STEPS - 3, kind).wait_send()
        z_forward(STEPS - 1, kind).start()
    add_all(end - 2)
    far(end, 0, 2)
    multiply(end, (0, 2))
    send_entries(entry_copies(end, end, EARLY))
    far(end, 2, 3)
    multiply(end, (2, 3), [(end + 1, LATE)] * 2)
    add_all(end - 1)
    add_early()
    make_late_hits()

    for q in range(2):
        entries_arrived(end + 1, end, LATE, q)
        add_late(q)
        for p in (2 * q, 2 * q + 1):
            at = slice((p % 2) * OWN, (p % 2 + 1) * OWN)
            for i in (2, 1, 3):
                s2[p, i - 1] = acc2[q, (b + i) % SIDE, :, at].astype(BF16)
                b_copy(i, p).start()
    for p in range(4):
        for i in range(1, SIDE):
            b_copy(i, p).wait_recv()
        at = slice((p % 2) * OWN, (p % 2 + 1) * OWN)
        total = acc2[p // 2, b, :, at] + (r2[p, 0].astype(F32) + r2[p, 1].astype(F32) + r2[p, 2].astype(F32))
        tot[p] = total
        for cc in range(2):
            fsum[p, cc] = total[cc * OWN : (cc + 1) * OWN, :].astype(BF16)
        for c in last_copies(p):
            c.start()
        own[core, p] = tot[p, pl.ds(pl.multiple_of(core * OWN, OWN), OWN), :]
    pick = (lax.broadcasted_iota(I32, (OWN, OWN), 0) == mp_ref[...]).astype(F32).astype(BF16)
    flip = (
        lax.broadcasted_iota(I32, (OWN, OWN), 0) + lax.broadcasted_iota(I32, (OWN, OWN), 1) == OWN - 1
    ).astype(F32).astype(BF16)
    for p in range(4):
        remote(own.at[0, p], own.at[0, p], fs_sem.at[p, 2], fr_sem.at[p, 2], sib).wait_recv()
        for h in range(2):
            ref = mir_in.at[h, p]
            remote(ref, ref, fs_sem.at[p, 0], fr_sem.at[p, h], dev(x, y, 0, z_far)).wait_recv()
        for h in range(2):
            rows = lax.dot_general(
                pick, mir_in[1 - h, p], (((0,), (0,)), ((), ())), preferred_element_type=F32
            ).astype(BF16)
            at = h * HALF + (3 - p) * OWN
            out_ref[0, :, at : at + OWN] = jnp.dot(rows, flip, preferred_element_type=F32)
    for p in range(4):
        for h in range(2):
            at = slice(h * HALF + p * OWN, h * HALF + (p + 1) * OWN)
            out_ref[0, :, at] = 0.5 * (own[h, p] + out_ref[0, :, at])

    halo_up.wait_send()
    halo_down.wait_send()
    for c in pos_copies:
        c.wait_send()

    @pl.loop(0, STEPS)
    def _(t):
        for kind in range(2):
            z_direct(t, kind).wait_send()

        @pl.when(t != STEPS - 3)
        def _():
            for kind in range(2):
                z_forward(t, kind).wait_send()

    @pl.loop(0, end)
    def _(t):
        for q in range(2):
            for c in entry_copies(t, t, ALL, q):
                c.wait_send()

    for c in entry_copies(end, end, EARLY):
        c.wait_send()
    for q in range(2):
        for c in entry_copies(end + 1, end, LATE, q):
            c.wait_send()

    for p in range(4):
        for i in range(1, SIDE):
            b_copy(i, p).wait_send()
        for c in last_copies(p):
            c.wait_send()


def shards(frame_pixels, bragg_mask, interp, block_list, owner_map, mirror_pair):
    vmem = pl.BlockSpec(memory_space=pltpu.VMEM)
    hbm = pl.BlockSpec(memory_space=pl.ANY)
    dma = pltpu.SemaphoreType.DMA
    return pl.pallas_call(
        kernel,
        out_shape=jax.ShapeDtypeStruct((1, OWN, VOX), F32),
        in_specs=[hbm, hbm, hbm, vmem, vmem, vmem],
        out_specs=vmem,
        scratch_shapes=[
            pltpu.VMEM((FRAMES, ROWS + 16, COLS), F32),
            pltpu.VMEM((FRAMES, ROWS, COLS), I32),
            pltpu.VMEM((4, PIX, QUART), BF16),
            pltpu.VMEM((8, FRAMES * BAND, 128), F32),
            pltpu.VMEM((UNITS, 3, PART, PIX), BF16),
            pltpu.VMEM((ENTRIES, QUART), F32),
            pltpu.VMEM((UNITS, 2, ENTRIES, QUART), BF16),
            pltpu.VMEM((UNITS, 2, 2 * SIDE, ENTRIES, QUART), BF16),
            pltpu.VMEM((2, SIDE, 256, QUART), F32),
            pltpu.VMEM((SIDE, 256, 2 * SIDE * ENTRIES), BF16),
            pltpu.VMEM((32, 128), I32),
            pltpu.VMEM((8, 128), I32),
            pltpu.VMEM((2 * SIDE, 8, 128), I32),
            pltpu.VMEM((8, 2 * SIDE * ENTRIES), I32),
            pltpu.VMEM((8, 4 * SIDE * PART), I32),
            pltpu.VMEM((8, 2 * SIDE * PART), I32),
            pltpu.VMEM((SIDE * 256, 2 * SIDE * PART), BF16),
            pltpu.VMEM((2, FRAMES // 2, 8, COLS), F32),
            pltpu.VMEM((2, FRAMES // 2, 8, COLS), F32),
            pltpu.VMEM((4, 3, 256, OWN), BF16),
            pltpu.VMEM((4, 3, 256, OWN), BF16),
            pltpu.VMEM((4, 2, OWN, OWN), BF16),
            pltpu.VMEM((4, 256, OWN), F32),
            pltpu.VMEM((2, 4, OWN, OWN), BF16),
            pltpu.VMEM((2, 4, OWN, OWN), F32),
            dma((4,)),
            dma((4,)),
            dma((2,)),
            dma((2,)),
            dma((7,)),
            dma((8,)),
            dma((STEPS, 4)),
            dma((STEPS, 4)),
            dma((UNITS + 1, 2, 7)),
            dma((UNITS + 1, 2, 8)),
            dma((4, 3)),
            dma((4, 3)),
            dma((4, 3)),
            dma((4, 3)),
        ],
        compiler_params=pltpu.CompilerParams(
            collective_id=0, has_side_effects=True, vmem_limit_bytes=60 * 1024 * 1024
        ),
    )(frame_pixels, bragg_mask, interp, block_list, owner_map, mirror_pair)


def solution(mesh):
    return jax.shard_map(
        shards,
        mesh=mesh,
        in_specs=(
            P("frames", "slabs", None),
            P("frames", "slabs", None),
            P("slabs", None, None),
            P("frames", "slabs", None),
            P("slabs", None),
            P("slabs", None),
        ),
        out_specs=P("slabs", "frames", None),
        check_vma=False,
    )
```
